256 devices in a mesh: row: 8 (over x, core), col: 32 (over z, y).
Axes of the slice: x: 4, y: 4, z: 8, core: 2. Of those that a mesh axis runs over, the one named last changes fastest.
Arguments:
- picture_embedding_matrix: bfloat16 [16384, 1152], P(('row', 'col')), may hold values from -0.19921875 to 0.19921875
- caption_embedding_matrix: bfloat16 [16384, 1152], P(('row', 'col')), may hold values from -0.19921875 to 0.19921875
- sharpness_scale: float32 [1], replicated, may hold values from 4 to 12
- additive_shift: float32 [1], replicated, may hold values from -4 to -2
Outputs:
- grad_images: float32 [16384, 1152], P(('row', 'col'))
- grad_texts: float32 [16384, 1152], P(('row', 'col'))
- image_loss: float32 [16384], P(('row', 'col'))
The draws below stay inside these ranges and needn't reach their ends.
All inputs are finite; a program needn't handle non-finite values.
Results may differ from the reference program's by a relative error of at most 0.0053.
Values may be sent and summed in bfloat16 or wider, within the bound.
No kernel may reach another device: no remote copies, remote signals or barrier semaphores. Data moves between devices by JAX's collectives and lax.ppermute only.
A program may use at most 128 MiB of HBM per device.

```python
import jax
import jax.numpy as jnp
from jax import lax

D = 1152
ROWS_DEV = 64
BATCH = 16384
N_COL = 32


def block_levels(rng, extent, pieces, least, high):
    level, own = 1.0, jax.random.fold_in(rng, 6)
    for position, shards_of in pieces:
        heights = jnp.exp(jax.random.uniform(jax.random.fold_in(own, position), (shards_of,), jnp.float32, least / len(pieces), high / len(pieces)))
        level = level * jnp.repeat(heights, extent[position] // shards_of).reshape([-1 if axis == position else 1 for axis in range(len(extent))])
    return level


def scatter_about(rng, extent, spread, most, split=(), kind=jnp.bfloat16):
    entries = spread * jax.random.normal(rng, extent, jnp.float32)
    if split:
        entries = entries * block_levels(rng, extent, split, -0.22, 0.18)
    return jnp.clip(entries, -most, most).astype(kind)


def setup_inputs(seed: int = 0) -> dict:
    splits = jax.random.split(jax.random.key(seed), 5)
    return {
        "picture_embedding_matrix": scatter_about(splits[0], (BATCH, D), 0.03, 0.19921875, ((0, 256),)),
        "caption_embedding_matrix": scatter_about(splits[1], (BATCH, D), 0.03, 0.19921875, ((0, 256),)),
        "sharpness_scale": jnp.clip(jax.random.uniform(splits[2], (1,), jnp.float32, 4.0, 12.0), 4.0, 12.0),
        "additive_shift": jnp.clip(jax.random.uniform(splits[3], (1,), jnp.float32, -4.0, -2.0), -4.0, -2.0),
    }


EPS = 1e-06

def normalize(feats):
    values = feats.astype(jnp.float32)
    inverse = lax.rsqrt(lax.optimization_barrier(jnp.sum(values * values, axis=-1, keepdims=True)) + EPS)
    return (values * inverse, inverse)

def back_norm(grad, unit, inverse):
    return inverse * (grad - unit * lax.optimization_barrier(jnp.sum(unit * grad, axis=-1, keepdims=True)))

def reference(picture_embedding_matrix, caption_embedding_matrix, sharpness_scale, additive_shift):
    img_f, img_inv = normalize(picture_embedding_matrix)
    txt_f, txt_inv = normalize(caption_embedding_matrix)
    img_b = img_f.astype(jnp.bfloat16)
    caption_segment = txt_f.astype(jnp.bfloat16)
    block = ROWS_DEV * N_COL
    blocks = BATCH // block
    columns = jnp.arange(BATCH, dtype=jnp.int32)

    def step(acc, index):
        start = (index * block).astype(jnp.int32)
        sample_total = lax.dynamic_slice_in_dim(img_b, start, block, 0)
        similarity_matrix = jnp.dot(sample_total, caption_segment.T, preferred_element_type=jnp.float32) * sharpness_scale[0] + additive_shift[0]
        ids = start + jnp.arange(block, dtype=jnp.int32)
        match_sign = ids[:, None] == columns[None, :]
        label = jnp.where(match_sign, jnp.float32(1.0), jnp.float32(-1.0))
        sigmoid_loss = lax.optimization_barrier(jnp.sum(jnp.log1p(jnp.exp(-label * similarity_matrix)), axis=1))
        logistic_weight = (sharpness_scale[0] * (jax.nn.sigmoid(similarity_matrix) - match_sign.astype(jnp.float32))).astype(jnp.bfloat16)
        g_rows = jnp.dot(logistic_weight, caption_segment, preferred_element_type=jnp.float32)
        acc = acc + lax.dot_general(logistic_weight, sample_total, (((0,), (0,)), ((), ())), preferred_element_type=jnp.float32)
        return (acc, (g_rows, sigmoid_loss))
    start_acc = jnp.zeros((BATCH, D), jnp.float32)
    g_txt, (g_img, sigmoid_loss) = lax.scan(step, start_acc, jnp.arange(blocks, dtype=jnp.int32))
    g_img = g_img.reshape(BATCH, D)
    sigmoid_loss = sigmoid_loss.reshape(BATCH)
    return (back_norm(g_img, img_f, img_inv), back_norm(g_txt, txt_f, txt_inv), sigmoid_loss)
```

```python
import functools

import jax
import jax.numpy as jnp
from jax import lax
from jax.experimental import pallas as pl
from jax.experimental.pallas import tpu as pltpu
from jax.sharding import Mesh
from jax.sharding import PartitionSpec as P

AXES = ("x", "core", "z", "y")
NX, NC, NZ, NY = 4, 2, 8, 4
EPS = 1e-06
F32 = jnp.float32
BF16 = jnp.bfloat16
MIB = 1 << 20
VMEM = pl.BlockSpec(memory_space=pltpu.VMEM)
SMEM = pl.BlockSpec(memory_space=pltpu.SMEM)


def device(x, core, z, y):
    return ((x % NX * NC + core) * NZ + z % NZ) * NY + y % NY


def permutation(move):
    return [
        (device(x, c, z, y), device(*move(x, c, z, y)))
        for x in range(NX)
        for c in range(NC)
        for z in range(NZ)
        for y in range(NY)
    ]


def first(a, s):
    return lax.ppermute(
        a, AXES, permutation(lambda x, c, z, y: (x, c, z, y + s) if c else (x + s, c, z, y))
    )


def second(a, s):
    return lax.ppermute(
        a, AXES, permutation(lambda x, c, z, y: (x + s, c, z, y) if c else (x, c, z, y + s))
    )


def along_z(a, s):
    return lax.ppermute(a, AXES, permutation(lambda x, c, z, y: (x, c, z + s, y)))


def swap_core(a):
    return lax.ppermute(a, AXES, permutation(lambda x, c, z, y: (x, 1 - c, z, y)))


def call(body, outs, n_in, flops, moved, name, scalars=0):
    return pl.pallas_call(
        body,
        out_shape=outs,
        in_specs=[SMEM] * scalars + [VMEM] * (n_in - scalars),
        out_specs=[VMEM] * len(outs),
        name=name,
        cost_estimate=pl.CostEstimate(flops=flops, bytes_accessed=moved, transcendentals=0),
        compiler_params=pltpu.CompilerParams(vmem_limit_bytes=20 * MIB),
    )


def shape(*dims, dtype=BF16):
    return jax.ShapeDtypeStruct(dims, dtype)


def normalize_body(img_ref, txt_ref, img_unit, txt_unit, img_inv, txt_inv):
    for raw, unit, inv in ((img_ref, img_unit, img_inv), (txt_ref, txt_unit, txt_inv)):
        v = raw[...].astype(F32)
        r = lax.rsqrt(jnp.sum(v * v, axis=-1, keepdims=True) + EPS)
        unit[...] = (v * r).astype(BF16)
        inv[...] = r


def split3(v):
    hi = v.astype(BF16).astype(F32)
    mid = (v - hi).astype(BF16).astype(F32)
    return hi, mid, v - hi - mid


def loss_rows(total):
    hi, mid, low = split3(total)
    at = lax.broadcasted_iota(jnp.int32, total.shape, 0)
    return jnp.where(at == 0, hi, jnp.where(at == 1, mid, jnp.where(at == 2, low, 0.0))).astype(BF16)


def loss_sum(rows):
    return jnp.sum(rows.astype(F32), axis=0, keepdims=True)


def entry_body(own, scale_ref, bias_ref, img_ref, txt_ref, coeff_ref, grad_ref, loss_ref=None):
    scale, bias = scale_ref[0], bias_ref[0]
    rows, cols = img_ref.shape[0], txt_ref.shape[0]
    step = 256
    total = jnp.zeros((rows, step), F32)
    for n in range(cols // step):
        at = slice(n * step, (n + 1) * step)
        dots = lax.dot_general(
            img_ref[...], txt_ref[at, :], (((1,), (1,)), ((), ())), preferred_element_type=F32
        )
        logits = dots * scale + bias
        if own and n == 0:
            r = lax.broadcasted_iota(jnp.int32, logits.shape, 0)
            c = lax.broadcasted_iota(jnp.int32, logits.shape, 1)
            match = (r == c) & (r < 64)
            e = jnp.exp(jnp.where(match, -logits, logits))
        else:
            e = jnp.exp(logits)
        u = 1.0 + e
        inv = 1.0 / u
        total = total + (jnp.log(u) + (e - (u - 1.0)) * inv)
        if own and n == 0:
            weight = jnp.where(match, -scale, scale) * (e * inv)
        else:
            weight = scale * (e * inv)
        coeff_ref[:, at] = weight.astype(BF16)
    grad = jnp.dot(coeff_ref[...], txt_ref[...], preferred_element_type=F32)
    loss = jnp.sum(total, axis=1, keepdims=True)
    across = jnp.transpose(jnp.broadcast_to(loss, (rows, 128)))[:8, :]
    if loss_ref is not None:
        grad_ref[...] = grad
        loss_ref[...] = across
    else:
        grad_ref[:rows, :] = grad.astype(BF16)
        grad_ref[rows:, :] = jnp.zeros((8, grad.shape[1]), BF16)
        grad_ref[rows:, :rows] = loss_rows(across)


def texts_body(c0, c1, c2, c3, s0, s1, s2, s3, out_ref, *, half):
    n = out_ref.shape[0]
    at = slice(half * n, (half + 1) * n)
    total = None
    for c, s in ((c0, s0), (c1, s1), (c2, s2), (c3, s3)):
        part = lax.dot_general(
            c[:, at], s[...], (((0,), (0,)), ((), ())), preferred_element_type=F32
        )
        total = part if total is None else total + part
    out_ref[...] = total.astype(out_ref.dtype)


def merge_img_body(g_ref, l_ref, r1, r2, r3, own_ref, own_loss, m1, m2, m3):
    rows = g_ref.shape[0]
    loss = l_ref[...] + (
        loss_sum(r1[rows:, :rows]) + loss_sum(r2[rows:, :rows]) + loss_sum(r3[rows:, :rows])
    )
    own_loss[...] = loss
    marks = loss_rows(loss)
    for j, out in enumerate((own_ref, m1, m2, m3)):
        at = slice(64 * j, 64 * j + 64)
        total = g_ref[at, :] + (
            r1[at, :].astype(F32) + r2[at, :].astype(F32) + r3[at, :].astype(F32)
        )
        out[:64, :] = total.astype(out.dtype)
        if j:
            out[64:, :] = jnp.zeros((8, total.shape[1]), BF16)
            out[64:, :rows] = marks


def merge_txt_body(g_ref, o_ref, a_ref, b_ref, far_a, far_b, near_ref):
    del a_ref, b_ref
    far_a[...] = (g_ref[256:384, :] + o_ref[256:384, :].astype(F32)).astype(BF16)
    far_b[...] = (g_ref[384:512, :] + o_ref[384:512, :].astype(F32)).astype(BF16)
    near_ref[...] = g_ref[:256, :] + o_ref[:256, :].astype(F32)


def merge_near_body(near_ref, a_ref, b_ref, own, back, ahead, across):
    own[...] = near_ref[:64, :]
    back[...] = (near_ref[64:128, :] + a_ref[:64, :].astype(F32)).astype(BF16)
    ahead[...] = (near_ref[128:192, :] + b_ref[:64, :].astype(F32)).astype(BF16)
    across[...] = (
        near_ref[192:256, :] + (a_ref[64:, :].astype(F32) + b_ref[64:, :].astype(F32))
    ).astype(BF16)


def back_norm(g, raw, inv):
    unit = raw[...].astype(F32) * inv[...]
    return inv[...] * (g - unit * jnp.sum(unit * g, axis=-1, keepdims=True))


def finish_img_body(g_ref, l_ref, r1, r2, r3, raw, inv, out_ref, loss_ref):
    g = g_ref[...] + (
        r1[:64, :].astype(F32) + r2[:64, :].astype(F32) + r3[:64, :].astype(F32)
    )
    out_ref[...] = back_norm(g, raw, inv)
    loss = l_ref[:1, :64]
    for j, r in enumerate((r1, r2, r3)):
        loss = loss + loss_sum(r[64:, 64 * (j + 1) : 64 * (j + 2)])
    loss_ref[...] = loss


def finish_txt_body(g_ref, r1, r2, r3, raw, inv, out_ref):
    g = g_ref[...] + (r1[...].astype(F32) + r2[...].astype(F32) + r3[...].astype(F32))
    out_ref[...] = back_norm(g, raw, inv)


def on_device(picture, caption, scale, bias):
    rows, d = picture.shape
    img, txt, img_inv, txt_inv = call(
        normalize_body,
        [shape(rows, d), shape(rows, d), shape(rows, 1, dtype=F32), shape(rows, 1, dtype=F32)],
        2, 0, 4 * rows * d * 2, "normalize",
    )(picture, caption)

    f1, f3, f2 = first(img, 1), first(img, 3), first(img, 2)
    t_back, t_ahead = along_z(txt, 1), along_z(txt, -1)
    t_across = along_z(txt, 4)
    group = jnp.concatenate([img, f1, f2, f3], axis=0)
    g1, g3, g2 = second(group, 1), second(group, 3), second(group, 2)
    groups = (group, g1, g2, g3)
    m_back = along_z(jnp.concatenate([t_back, t_across], axis=0), 1)
    m_ahead = along_z(jnp.concatenate([t_ahead, t_across], axis=0), -1)
    near = jnp.concatenate([txt, t_back, t_ahead, t_across], axis=0)
    far = jnp.concatenate([m_back, m_ahead], axis=0)
    texts = jnp.concatenate([near, far, swap_core(near), swap_core(far)], axis=0)

    n = texts.shape[0]
    m = group.shape[0]
    coeffs, grads = [], []
    cost = (4 * m * n * d, (2 * m * d + n * d + m * n) * 2)
    for k in (0, 1, 3, 2):
        outs = [shape(m, n)]
        if k == 0:
            outs += [shape(m, d, dtype=F32), shape(8, m, dtype=F32)]
        else:
            outs += [shape(m + 8, d)]
        res = call(functools.partial(entry_body, k == 0), outs, 4, *cost, f"entry{k}", scalars=2)(
            scale, bias, groups[k], texts
        )
        coeffs.append(res[0])
        grads.append(res[1:])
    order = (0, 1, 3, 2)
    by = [groups[k] for k in order]
    halves = [
        call(
            functools.partial(texts_body, half=h),
            [shape(n // 2, d, dtype=F32 if h == 0 else BF16)],
            8, m * 4 * n * d, (4 * m * d + 2 * m * n + n * d) * 2, f"texts{h}",
        )(*coeffs, *by)[0]
        for h in (1, 0)
    ]
    other, mine = halves

    r1, r3, r2 = second(grads[1][0], -1), second(grads[2][0], -3), second(grads[3][0], -2)
    own_img, own_loss, p1, p2, p3 = call(
        merge_img_body,
        [shape(rows, d, dtype=F32), shape(8, m, dtype=F32)] + [shape(rows + 8, d)] * 3,
        5, 0, 10 * m * d, "merge_img",
    )(*grads[0], r1, r2, r3)
    q1, q3, q2 = first(p1, -1), first(p3, -3), first(p2, -2)

    got = swap_core(other)
    far_a, far_b, near_f = call(
        lambda g, o, a, b, c: merge_txt_body(g, o, None, None, a, b, c),
        [shape(2 * rows, d), shape(2 * rows, d), shape(4 * rows, d, dtype=F32)],
        2, 0, 8 * rows * d * 8, "merge_txt",
    )(mine, got)
    a, b = along_z(far_a, -1), along_z(far_b, 1)
    own_txt, back, ahead, across = call(
        merge_near_body,
        [shape(rows, d, dtype=F32)] + [shape(rows, d)] * 3,
        3, 0, 4 * rows * d * 8, "merge_near",
    )(near_f, a, b)
    u1, u2, u3 = along_z(back, -1), along_z(ahead, 1), along_z(across, 4)

    grad_img, loss = call(
        finish_img_body,
        [shape(rows, d, dtype=F32), shape(1, rows, dtype=F32)],
        7, 0, rows * d * 16, "finish_img",
    )(own_img, own_loss, q1, q2, q3, picture, img_inv)
    grad_txt = call(
        finish_txt_body, [shape(rows, d, dtype=F32)], 6, 0, rows * d * 16, "finish_txt"
    )(own_txt, u1, u2, u3, caption, txt_inv)[0]
    return grad_img, grad_txt, loss.reshape(rows)


def solution(mesh):
    torus = Mesh(mesh.devices.reshape(NX, NC, NZ, NY), AXES)
    return jax.shard_map(
        on_device,
        mesh=torus,
        in_specs=(P(AXES, None), P(AXES, None), P(), P()),
        out_specs=(P(AXES, None), P(AXES, None), P(AXES)),
        check_vma=False,
    )
```

```python
import functools

import jax
import jax.numpy as jnp
from jax import lax
from jax.experimental import pallas as pl
from jax.experimental.pallas import tpu as pltpu
from jax.sharding import Mesh
from jax.sharding import PartitionSpec as P

AXES = ("x", "core", "z", "y")
NX, NC, NZ, NY = 4, 2, 8, 4
U = 64
EPS = 1e-06
F32 = jnp.float32
BF16 = jnp.bfloat16
MIB = 1 << 20
VMEM = pl.BlockSpec(memory_space=pltpu.VMEM)
SMEM = pl.BlockSpec(memory_space=pltpu.SMEM)
ANY = pl.BlockSpec(memory_space=pl.ANY)
HBM = pl.BlockSpec(memory_space=pltpu.HBM)


def device(x, core, z, y):
    return ((x % NX * NC + core) * NZ + z % NZ) * NY + y % NY


def permutation(move):
    return [
        (device(x, c, z, y), device(*move(x, c, z, y)))
        for x in range(NX)
        for c in range(NC)
        for z in range(NZ)
        for y in range(NY)
    ]


def first(a, s):
    return lax.ppermute(
        a, AXES, permutation(lambda x, c, z, y: (x, c, z, y + s) if c else (x + s, c, z, y))
    )


def second(a, s):
    return lax.ppermute(
        a, AXES, permutation(lambda x, c, z, y: (x + s, c, z, y) if c else (x, c, z, y + s))
    )


def ring(a, s):
    return lax.ppermute(a, AXES, permutation(lambda x, c, z, y: (x, c, z - s if c else z + s, y)))


def swap(a):
    return lax.ppermute(a, AXES, permutation(lambda x, c, z, y: (x, 1 - c, z, y)))


def call(name, body, outs, ins, scalars=(), after=(), specs=None, scratch=()):
    n_out, n_in = len(outs), len(ins) + len(scalars)

    def kernel(*refs):
        used = refs[:n_in] + refs[n_in + len(after) :]
        body(*used)

    return pl.pallas_call(
        kernel,
        out_shape=outs,
        in_specs=[SMEM] * len(scalars) + (specs or [VMEM] * len(ins)) + [ANY] * len(after),
        out_specs=[VMEM] * n_out,
        scratch_shapes=list(scratch),
        name=name,
        cost_estimate=pl.CostEstimate(flops=1, bytes_accessed=1, transcendentals=0),
        compiler_params=pltpu.CompilerParams(vmem_limit_bytes=20 * MIB),
    )(*scalars, *ins, *after)


def shape(*dims, dtype=BF16):
    return jax.ShapeDtypeStruct(dims, dtype)


def up(ref, lo, hi):
    return ref[lo:hi, :].astype(F32)


def normalize_body(img_ref, txt_ref, img_unit, txt_unit, img_inv, txt_inv, raw_ref, sem):
    copies = [
        pltpu.make_async_copy(src, raw_ref.at[i], sem.at[i])
        for i, src in enumerate((img_ref, txt_ref))
    ]
    for copy in copies:
        copy.start()
    for i, (unit, inv) in enumerate(((img_unit, img_inv), (txt_unit, txt_inv))):
        copies[i].wait()
        v = raw_ref[i].astype(F32)
        r = lax.rsqrt(jnp.sum(v * v, axis=-1, keepdims=True) + EPS)
        unit[...] = (v * r).astype(BF16)
        inv[...] = r


def split3(v):
    hi = v.astype(BF16).astype(F32)
    mid = (v - hi).astype(BF16).astype(F32)
    return hi, mid, v - hi - mid


def loss_rows(total):
    hi, mid, low = split3(total)
    at = lax.broadcasted_iota(jnp.int32, total.shape, 0)
    return jnp.where(at == 0, hi, jnp.where(at == 1, mid, jnp.where(at == 2, low, 0.0))).astype(BF16)


def loss_sum(rows):
    return jnp.sum(rows.astype(F32), axis=0, keepdims=True)


def entry(img, txt, scale, bias, match=None):
    dots = lax.dot_general(img, txt, (((1,), (1,)), ((), ())), preferred_element_type=F32)
    logits = dots * scale + bias
    if match is not None:
        logits = jnp.where(match, -logits, logits)
    e = jnp.exp(logits)
    u = 1.0 + e
    inv = 1.0 / u
    softplus = jnp.log(u) + (e - (u - 1.0)) * inv
    weight = scale * (e * inv)
    if match is not None:
        weight = jnp.where(match, -weight, weight)
    return weight.astype(BF16), softplus


def fold(v):
    total = v[:, :128]
    for n in range(1, v.shape[1] // 128):
        total = total + v[:, 128 * n : 128 * (n + 1)]
    return total


def near_body(scale_ref, bias_ref, img_ref, txt_ref, coeff_ref, loss_ref):
    total = None
    for n in range(2):
        at = slice(256 * n, 256 * (n + 1))
        weight, softplus = entry(img_ref[...], txt_ref[at, :], scale_ref[0], bias_ref[0])
        coeff_ref[:, at] = weight
        total = fold(softplus) if total is None else total + fold(softplus)
    loss_ref[...] = total


def texts(coeffs, imgs, lo, hi):
    total = None
    for c, s in zip(coeffs, imgs):
        part = lax.dot_general(
            c[:, lo:hi], s[...], (((0,), (0,)), ((), ())), preferred_element_type=F32
        )
        total = part if total is None else total + part
    return total


def far_body(scale_ref, bias_ref, i0, i1, i2, i3, txt_ref, l0, l1, l2, l3, c0, c1, c2, c3, keep, send, pair, loss):
    scale, bias = scale_ref[0], bias_ref[0]
    imgs, coeffs, sums = (i0, i1, i2, i3), (c0, c1, c2, c3), (l0, l1, l2, l3)
    for k in range(4):
        total = sums[k][...]
        for n in range(2):
            at = slice(256 * n, 256 * (n + 1))
            match = None
            if k == 0 and n == 1:
                r = lax.broadcasted_iota(jnp.int32, (256, 256), 0)
                c = lax.broadcasted_iota(jnp.int32, (256, 256), 1)
                match = (r + 128 == c) & (r < U)
            weight, softplus = entry(imgs[k][...], txt_ref[at, :], scale, bias, match)
            coeffs[k][:, at] = weight
            total = total + fold(softplus)
        column = jnp.broadcast_to(jnp.sum(total, axis=1, keepdims=True), (256, 128))
        loss[:, 256 * k : 256 * (k + 1)] = jnp.transpose(column)[:8, :]
    g = texts(coeffs, imgs, 0, 256)
    keep[...] = g[:192, :]
    send[:64, :] = g[192:, :].astype(BF16)
    g = texts(coeffs, imgs, 256, 512)
    send[64:, :] = g[:128, :].astype(BF16)
    pair[...] = g[128:, :]


def near_texts_body(c0, c1, c2, c3, i0, i1, i2, i3, keep, send):
    coeffs, imgs = (c0, c1, c2, c3), (i0, i1, i2, i3)
    keep[...] = texts(coeffs, imgs, 0, 256)
    send[...] = texts(coeffs, imgs, 256, 512).astype(BF16)


def image_body(k, cf, cn, far, near, loss, out):
    g = jnp.dot(cf[...], far[...], preferred_element_type=F32)
    g = g + jnp.dot(cn[...], near[...], preferred_element_type=F32)
    if k == 0:
        out[...] = g
    else:
        out[:256, :] = g.astype(BF16)
        out[256:, :] = jnp.zeros((8, g.shape[1]), BF16)
        out[256:, :256] = loss_rows(loss[:, 256 * k : 256 * (k + 1)])


def merge_img_body(g_ref, l_ref, r1, r2, r3, own_ref, own_loss, m1, m2, m3):
    loss = l_ref[:, :256] + (
        loss_sum(r1[256:, :256]) + loss_sum(r2[256:, :256]) + loss_sum(r3[256:, :256])
    )
    own_loss[...] = loss
    marks = loss_rows(loss)
    for j, out in enumerate((own_ref, m1, m2, m3)):
        lo, hi = U * j, U * (j + 1)
        total = g_ref[lo:hi, :] + (up(r1, lo, hi) + up(r2, lo, hi) + up(r3, lo, hi))
        out[:U, :] = total.astype(out.dtype)
        if j:
            out[U:, :] = jnp.zeros((8, total.shape[1]), BF16)
            out[U:, :256] = marks


def step1_body(keep, got, out):
    out[...] = (keep[:64, :] + up(got, 0, 64)).astype(BF16)


def step2_body(keep, got, r, out):
    out[:64, :] = (keep[64:128, :] + (up(got, 64, 128) + up(r, 0, 64))).astype(BF16)
    out[64:, :] = (keep[128:192, :] + up(got, 128, 192)).astype(BF16)


def step_body(lo, keep, got, r, out):
    hi = lo + 128
    out[...] = (keep[lo:hi, :] + (up(got, lo, hi) + up(r, 0, 128))).astype(BF16)


def step5_body(pair, r, out):
    out[...] = (pair[64:, :] + up(r, 64, 128)).astype(BF16)


def back_norm(g, raw, inv):
    unit = raw[...].astype(F32) * inv[...]
    return inv[...] * (g - unit * jnp.sum(unit * g, axis=-1, keepdims=True))


def finish_img_body(g_ref, l_ref, r1, r2, r3, raw, inv, out_ref, loss_ref):
    g = g_ref[...] + (up(r1, 0, U) + up(r2, 0, U) + up(r3, 0, U))
    out_ref[...] = back_norm(g, raw, inv)
    loss = l_ref[:1, :U]
    for j, r in enumerate((r1, r2, r3)):
        loss = loss + loss_sum(r[U:, U * (j + 1) : U * (j + 2)])
    loss_ref[...] = loss


def finish_txt_body(pair, r, got, raw, inv, out_ref):
    g = pair[:64, :] + (up(r, 0, 64) + got[...].astype(F32))
    out_ref[...] = back_norm(g, raw, inv)


def on_device(picture, caption, scale, bias):
    rows, d = picture.shape
    img, txt, img_inv, txt_inv = call(
        "normalize", normalize_body,
        [shape(rows, d), shape(rows, d), shape(rows, 1, dtype=F32), shape(rows, 1, dtype=F32)],
        [pltpu.with_memory_space_constraint(a, pltpu.HBM) for a in (picture, caption)], specs=[HBM] * 2,
        scratch=[pltpu.VMEM((2, rows, d), BF16), pltpu.SemaphoreType.DMA((2,))],
    )

    pair = jnp.concatenate([txt, swap(txt)], axis=0)
    f1, f3, f2 = first(img, 1), first(img, 3), first(img, 2)
    b1 = ring(pair, 1)
    group = jnp.concatenate([img, f1, f2, f3], axis=0)
    g1, g3, g2 = second(group, 1), second(group, 3), second(group, 2)
    groups = (group, g1, g2, g3)
    b2 = ring(b1, 1)
    near_mine = jnp.concatenate([b2, b1], axis=0)
    near = jnp.concatenate([near_mine, swap(near_mine)], axis=0)
    b3 = ring(b2, 1)
    b4 = ring(b3[:U], 1)
    far_mine = jnp.concatenate([b4, b3], axis=0)
    far = jnp.concatenate([far_mine, swap(far_mine), pair], axis=0)

    sc = (scale, bias)
    near_c, near_l, last = [None] * 4, [None] * 4, ()
    for k in (0, 1, 3, 2):
        near_c[k], near_l[k] = call(
            f"near{k}", near_body, [shape(256, 512), shape(256, 128, dtype=F32)],
            (groups[k], near), sc, last,
        )
        last = (near_l[k],)
    *far_c, keep_a, send_a, own_pair, loss = call(
        "far", far_body,
        [shape(256, 512)] * 4
        + [shape(192, d, dtype=F32), shape(192, d), shape(128, d, dtype=F32), shape(8, 1024, dtype=F32)],
        (*groups, far, *near_l), sc,
    )
    got_a = swap(send_a)

    def image(k, after):
        out = shape(256, d, dtype=F32) if k == 0 else shape(264, d)
        return call(
            f"image{k}", functools.partial(image_body, k), [out],
            (far_c[k], near_c[k], far, near, loss), (), after,
        )[0]

    keep_b, send_b = call(
        "near_texts", near_texts_body, [shape(256, d, dtype=F32), shape(256, d)],
        (*near_c, *groups), (), (send_a,),
    )
    got_b = swap(send_b)
    z1 = call("step1", step1_body, [shape(64, d)], (keep_a, got_a), (), (send_b,))[0]
    w1 = ring(z1, -1)
    p1 = image(1, (z1,))
    r1 = second(p1, -1)
    p3 = image(3, (p1,))
    r3 = second(p3, -3)
    z2 = call("step2", step2_body, [shape(128, d)], (keep_a, got_a, w1), (), (p3, got_b))[0]
    w2 = ring(z2, -1)
    p2 = image(2, (z2,))
    r2 = second(p2, -2)
    p0 = image(0, (p2,))
    z3 = call("step3", functools.partial(step_body, 0), [shape(128, d)], (keep_b, got_b, w2), (), (p0,))[0]
    w3 = ring(z3, -1)
    own_img, own_loss, m1, m2, m3 = call(
        "merge_img", merge_img_body,
        [shape(rows, d, dtype=F32), shape(8, 256, dtype=F32)] + [shape(rows + 8, d)] * 3,
        (p0, loss, r1, r2, r3), (), (z3,),
    )
    q1, q3, q2 = first(m1, -1), first(m3, -3), first(m2, -2)
    z4 = call("step4", functools.partial(step_body, 128), [shape(128, d)], (keep_b, got_b, w3), (), (m3,))[0]
    w4 = ring(z4, -1)
    z5 = call("step5", step5_body, [shape(64, d)], (own_pair, w4))[0]
    got_c = swap(z5)
    grad_img, loss_out = call(
        "finish_img", finish_img_body,
        [shape(rows, d, dtype=F32), shape(1, rows, dtype=F32)],
        (own_img, own_loss, q1, q2, q3, picture, img_inv), (), (z5,),
    )
    grad_txt = call(
        "finish_txt", finish_txt_body, [shape(rows, d, dtype=F32)],
        (own_pair, w4, got_c, caption, txt_inv),
    )[0]
    return grad_img, grad_txt, loss_out.reshape(rows)


def solution(mesh):
    torus = Mesh(mesh.devices.reshape(NX, NC, NZ, NY), AXES)
    return jax.shard_map(
        on_device,
        mesh=torus,
        in_specs=(P(AXES, None), P(AXES, None), P(), P()),
        out_specs=(P(AXES, None), P(AXES, None), P(AXES)),
        check_vma=False,
    )
```

```python
import functools

import jax
import jax.numpy as jnp
from jax import lax
from jax.experimental import pallas as pl
from jax.experimental.pallas import tpu as pltpu
from jax.sharding import Mesh
from jax.sharding import PartitionSpec as P

AXES = ("x", "core", "z", "y")
NX, NC, NZ, NY = 4, 2, 8, 4
U = 64
EPS = 1e-06
F32 = jnp.float32
BF16 = jnp.bfloat16
MIB = 1 << 20
VMEM = pl.BlockSpec(memory_space=pltpu.VMEM)
SMEM = pl.BlockSpec(memory_space=pltpu.SMEM)
ANY = pl.BlockSpec(memory_space=pl.ANY)
HBM = pl.BlockSpec(memory_space=pltpu.HBM)


def device(x, core, z, y):
    return ((x % NX * NC + core) * NZ + z % NZ) * NY + y % NY


def permutation(move):
    return [
        (device(x, c, z, y), device(*move(x, c, z, y)))
        for x in range(NX)
        for c in range(NC)
        for z in range(NZ)
        for y in range(NY)
    ]


def first(a, s):
    return lax.ppermute(
        a, AXES, permutation(lambda x, c, z, y: (x, c, z, y + s) if c else (x + s, c, z, y))
    )


def second(a, s):
    return lax.ppermute(
        a, AXES, permutation(lambda x, c, z, y: (x + s, c, z, y) if c else (x, c, z, y + s))
    )


def ring(a, s):
    return lax.ppermute(a, AXES, permutation(lambda x, c, z, y: (x, c, z - s if c else z + s, y)))


def swap(a):
    return lax.ppermute(a, AXES, permutation(lambda x, c, z, y: (x, 1 - c, z, y)))


def call(name, body, outs, ins, scalars=(), after=(), specs=None, scratch=()):
    n_out, n_in = len(outs), len(ins) + len(scalars)

    def kernel(*refs):
        used = refs[:n_in] + refs[n_in + len(after) :]
        body(*used)

    return pl.pallas_call(
        kernel,
        out_shape=outs,
        in_specs=[SMEM] * len(scalars) + (specs or [VMEM] * len(ins)) + [ANY] * len(after),
        out_specs=[VMEM] * n_out,
        scratch_shapes=list(scratch),
        name=name,
        cost_estimate=pl.CostEstimate(flops=1, bytes_accessed=1, transcendentals=0),
        compiler_params=pltpu.CompilerParams(vmem_limit_bytes=20 * MIB),
    )(*scalars, *ins, *after)


def shape(*dims, dtype=BF16):
    return jax.ShapeDtypeStruct(dims, dtype)


def up(ref, lo, hi):
    return ref[lo:hi, :].astype(F32)


def normalize_body(img_ref, txt_ref, img_unit, txt_unit, img_inv, txt_inv, raw_ref, sem):
    copies = [
        pltpu.make_async_copy(src, raw_ref.at[i], sem.at[i])
        for i, src in enumerate((img_ref, txt_ref))
    ]
    for copy in copies:
        copy.start()
    for i, (unit, inv) in enumerate(((img_unit, img_inv), (txt_unit, txt_inv))):
        copies[i].wait()
        v = raw_ref[i].astype(F32)
        r = lax.rsqrt(jnp.sum(v * v, axis=-1, keepdims=True) + EPS)
        unit[...] = (v * r).astype(BF16)
        inv[...] = r


def split3(v):
    hi = v.astype(BF16).astype(F32)
    mid = (v - hi).astype(BF16).astype(F32)
    return hi, mid, v - hi - mid


def loss_rows(total):
    hi, mid, low = split3(total)
    at = lax.broadcasted_iota(jnp.int32, total.shape, 0)
    return jnp.where(at == 0, hi, jnp.where(at == 1, mid, jnp.where(at == 2, low, 0.0))).astype(BF16)


def loss_sum(rows):
    return jnp.sum(rows.astype(F32), axis=0, keepdims=True)


def entry(img, txt, scale, bias, match=None):
    dots = lax.dot_general(img, txt, (((1,), (1,)), ((), ())), preferred_element_type=F32)
    logits = dots * scale + bias
    if match is not None:
        logits = jnp.where(match, -logits, logits)
    e = jnp.exp(logits)
    u = 1.0 + e
    inv = 1.0 / u
    softplus = jnp.log(u) + (e - (u - 1.0)) * inv
    weight = scale * (e * inv)
    if match is not None:
        weight = jnp.where(match, -weight, weight)
    return weight.astype(BF16), softplus


def fold(v):
    total = v[:, :128]
    for n in range(1, v.shape[1] // 128):
        total = total + v[:, 128 * n : 128 * (n + 1)]
    return total


def mine_body(scale_ref, bias_ref, img_ref, txt_ref, coeff_ref, loss_ref):
    weight, softplus = entry(img_ref[...], txt_ref[...], scale_ref[0], bias_ref[0])
    coeff_ref[...] = weight
    loss_ref[...] = fold(softplus)


def texts(coeffs, imgs, lo, hi):
    total = None
    for c, s in zip(coeffs, imgs):
        part = lax.dot_general(
            c[:, lo:hi], s[...], (((0,), (0,)), ((), ())), preferred_element_type=F32
        )
        total = part if total is None else total + part
    return total


def far_body(scale_ref, bias_ref, i0, i1, i2, i3, txt_ref, near_loss, c0, c1, c2, c3, keep, send, pair, loss):
    scale, bias = scale_ref[0], bias_ref[0]
    imgs, coeffs = (i0, i1, i2, i3), (c0, c1, c2, c3)
    for k in range(4):
        total = near_loss[256 * k : 256 * (k + 1), :]
        for n in range(2):
            at = slice(256 * n, 256 * (n + 1))
            match = None
            if k == 0 and n == 1:
                r = lax.broadcasted_iota(jnp.int32, (256, 256), 0)
                c = lax.broadcasted_iota(jnp.int32, (256, 256), 1)
                match = (r + 128 == c) & (r < U)
            weight, softplus = entry(imgs[k][...], txt_ref[at, :], scale, bias, match)
            coeffs[k][:, at] = weight
            total = total + fold(softplus)
        column = jnp.broadcast_to(jnp.sum(total, axis=1, keepdims=True), (256, 128))
        loss[:, 256 * k : 256 * (k + 1)] = jnp.transpose(column)[:8, :]
    g = texts(coeffs, imgs, 0, 256)
    keep[...] = g[:192, :]
    send[:64, :] = g[192:, :].astype(BF16)
    g = texts(coeffs, imgs, 256, 512)
    send[64:, :] = g[:128, :].astype(BF16)
    pair[...] = g[128:, :]


def other_body(scale_ref, bias_ref, i0, i1, i2, i3, c0, c1, c2, c3, txt_ref, l0, l1, l2, l3, o0, o1, o2, o3, keep, send, loss):
    imgs, sums, mine, other = (i0, i1, i2, i3), (l0, l1, l2, l3), (c0, c1, c2, c3), (o0, o1, o2, o3)
    for k in range(4):
        weight, softplus = entry(imgs[k][...], txt_ref[...], scale_ref[0], bias_ref[0])
        other[k][...] = weight
        loss[256 * k : 256 * (k + 1), :] = sums[k][...] + fold(softplus)
    send[...] = texts(other, imgs, 0, 256).astype(BF16)
    keep[...] = texts(mine, imgs, 0, 256)


def copy_body(src, dst):
    dst[...] = src[...]


def image_body(k, cf, cm, co, far, mine, other, loss, out):
    g = jnp.dot(cf[...], far[...], preferred_element_type=F32)
    g = g + jnp.dot(cm[...], mine[...], preferred_element_type=F32)
    g = g + jnp.dot(co[...], other[...], preferred_element_type=F32)
    if k == 0:
        out[...] = g
    else:
        out[:256, :] = g.astype(BF16)
        out[256:, :] = jnp.zeros((8, g.shape[1]), BF16)
        out[256:, :256] = loss_rows(loss[:, 256 * k : 256 * (k + 1)])


def merge_img_body(g_ref, l_ref, r1, r2, r3, own_ref, own_loss, m1, m2, m3):
    loss = l_ref[:, :256] + (
        loss_sum(r1[256:, :256]) + loss_sum(r2[256:, :256]) + loss_sum(r3[256:, :256])
    )
    own_loss[...] = loss
    marks = loss_rows(loss)
    for j, out in enumerate((own_ref, m1, m2, m3)):
        lo, hi = U * j, U * (j + 1)
        total = g_ref[lo:hi, :] + (up(r1, lo, hi) + up(r2, lo, hi) + up(r3, lo, hi))
        out[:U, :] = total.astype(out.dtype)
        if j:
            out[U:, :] = jnp.zeros((8, total.shape[1]), BF16)
            out[U:, :256] = marks


def pack_body(b1, b2, far, near):
    far[:U, :] = b2[:U, :]
    far[U:, :] = b1[...]
    near[:128, :] = b2[...]
    near[128:, :] = b1[...]


def step1_body(keep, got, out):
    out[...] = (keep[...] + got[...].astype(F32)).astype(BF16)


def step2_body(keep, got, w, two, one):
    two[:64, :] = (keep[:64, :] + (up(got, 0, 64) + up(w, 0, 64))).astype(BF16)
    two[64:, :] = (keep[64:128, :] + up(got, 64, 128)).astype(BF16)
    one[...] = (keep[128:, :] + (up(got, 128, 256) + up(w, 64, 192))).astype(BF16)


def step3_body(pair, v1, v2, out):
    out[...] = (pair[64:, :] + (up(v1, 64, 128) + up(v2, 64, 128))).astype(BF16)


def back_norm(g, raw, inv):
    unit = raw[...].astype(F32) * inv[...]
    return inv[...] * (g - unit * jnp.sum(unit * g, axis=-1, keepdims=True))


def finish_img_body(g_ref, l_ref, r1, r2, r3, raw, inv, out_ref, loss_ref):
    g = g_ref[...] + (up(r1, 0, U) + up(r2, 0, U) + up(r3, 0, U))
    out_ref[...] = back_norm(g, raw, inv)
    loss = l_ref[:1, :U]
    for j, r in enumerate((r1, r2, r3)):
        loss = loss + loss_sum(r[U:, U * (j + 1) : U * (j + 2)])
    loss_ref[...] = loss


def finish_txt_body(pair, v1, v2, got, raw, inv, out_ref):
    g = pair[:64, :] + (up(v1, 0, 64) + up(v2, 0, 64) + got[...].astype(F32))
    out_ref[...] = back_norm(g, raw, inv)


def on_device(picture, caption, scale, bias):
    rows, d = picture.shape
    img, txt, img_inv, txt_inv = call(
        "normalize", normalize_body,
        [shape(rows, d), shape(rows, d), shape(rows, 1, dtype=F32), shape(rows, 1, dtype=F32)],
        [pltpu.with_memory_space_constraint(a, pltpu.HBM) for a in (picture, caption)], specs=[HBM] * 2,
        scratch=[pltpu.VMEM((2, rows, d), BF16), pltpu.SemaphoreType.DMA((2,))],
    )

    pair = jnp.concatenate([txt, swap(txt)], axis=0)
    f1, f3, f2 = first(img, 1), first(img, 3), first(img, 2)
    b1, b2 = ring(pair, 1), ring(pair, 2)
    group = jnp.concatenate([img, f1, f2, f3], axis=0)
    g1, g3, g2 = second(group, 1), second(group, 3), second(group, 2)
    groups = (group, g1, g2, g3)
    far_pack, near_mine = call(
        "pack", pack_body, [shape(192, d), shape(256, d)], (b1, b2), (), (group,)
    )
    far_got = ring(far_pack, 2)
    near_other = swap(near_mine)

    sc = (scale, bias)
    mine_c, mine_l, last = [None] * 4, [None] * 4, ()
    for k in (0, 1, 3, 2):
        mine_c[k], mine_l[k] = call(
            f"mine{k}", mine_body, [shape(256, 256), shape(256, 128, dtype=F32)],
            (groups[k], near_mine), sc, last,
        )
        last = (mine_l[k],)
    *other_c, keep_b, send_b, near_loss = call(
        "other", other_body,
        [shape(256, 256)] * 4 + [shape(256, d, dtype=F32), shape(256, d), shape(1024, 128, dtype=F32)],
        (*groups, *mine_c, near_other, *mine_l), sc, last,
    )
    got_b = swap(send_b)
    far_mine = call("arrived", copy_body, [shape(192, d)], (far_got,), (), (send_b,))[0]
    far = jnp.concatenate([far_mine, swap(far_mine), pair], axis=0)
    *far_c, keep_a, send_a, own_pair, loss = call(
        "far", far_body,
        [shape(256, 512)] * 4
        + [shape(192, d, dtype=F32), shape(192, d), shape(128, d, dtype=F32), shape(8, 1024, dtype=F32)],
        (*groups, far, near_loss), sc,
    )
    got_a = swap(send_a)

    def image(k, after):
        out = shape(256, d, dtype=F32) if k == 0 else shape(264, d)
        return call(
            f"image{k}", functools.partial(image_body, k), [out],
            (far_c[k], mine_c[k], other_c[k], far, near_mine, near_other, loss), (), after,
        )[0]

    p1 = image(1, ())
    r1 = second(p1, -1)
    z1 = call("step1", step1_body, [shape(192, d)], (keep_a, got_a), (), (p1, got_b))[0]
    w = ring(z1, -2)
    p3 = image(3, (z1,))
    r3 = second(p3, -3)
    p2 = image(2, (p3,))
    r2 = second(p2, -2)
    p0 = image(0, (p2,))
    two, one = call("step2", step2_body, [shape(128, d)] * 2, (keep_b, got_b, w), (), (p0,))
    v1, v2 = ring(one, -1), ring(two, -2)
    own_img, own_loss, m1, m2, m3 = call(
        "merge_img", merge_img_body,
        [shape(rows, d, dtype=F32), shape(8, 256, dtype=F32)] + [shape(rows + 8, d)] * 3,
        (p0, loss, r1, r2, r3), (), (one,),
    )
    q1, q3, q2 = first(m1, -1), first(m3, -3), first(m2, -2)
    z3 = call("step3", step3_body, [shape(64, d)], (own_pair, v1, v2), (), (m3,))[0]
    got_c = swap(z3)
    grad_img, loss_out = call(
        "finish_img", finish_img_body,
        [shape(rows, d, dtype=F32), shape(1, rows, dtype=F32)],
        (own_img, own_loss, q1, q2, q3, picture, img_inv), (), (z3,),
    )
    grad_txt = call(
        "finish_txt", finish_txt_body, [shape(rows, d, dtype=F32)],
        (own_pair, v1, v2, got_c, caption, txt_inv),
    )[0]
    return grad_img, grad_txt, loss_out.reshape(rows)


def solution(mesh):
    torus = Mesh(mesh.devices.reshape(NX, NC, NZ, NY), AXES)
    return jax.shard_map(
        on_device,
        mesh=torus,
        in_specs=(P(AXES, None), P(AXES, None), P(), P()),
        out_specs=(P(AXES, None), P(AXES, None), P(AXES)),
        check_vma=False,
    )
```

```python
import functools

import jax
import jax.numpy as jnp
from jax import lax
from jax.experimental import pallas as pl
from jax.experimental.pallas import tpu as pltpu
from jax.sharding import Mesh
from jax.sharding import PartitionSpec as P

AXES = ("x", "core", "z", "y")
NX, NC, NZ, NY = 4, 2, 8, 4
U = 64
EPS = 1e-06
F32 = jnp.float32
BF16 = jnp.bfloat16
MIB = 1 << 20
VMEM = pl.BlockSpec(memory_space=pltpu.VMEM)
SMEM = pl.BlockSpec(memory_space=pltpu.SMEM)
ANY = pl.BlockSpec(memory_space=pl.ANY)
HBM = pl.BlockSpec(memory_space=pltpu.HBM)


def device(x, core, z, y):
    return ((x % NX * NC + core) * NZ + z % NZ) * NY + y % NY


def permutation(move):
    return [
        (device(x, c, z, y), device(*move(x, c, z, y)))
        for x in range(NX)
        for c in range(NC)
        for z in range(NZ)
        for y in range(NY)
    ]


def first(a, s):
    return lax.ppermute(
        a, AXES, permutation(lambda x, c, z, y: (x, c, z, y + s) if c else (x + s, c, z, y))
    )


def second(a, s):
    return lax.ppermute(
        a, AXES, permutation(lambda x, c, z, y: (x + s, c, z, y) if c else (x, c, z, y + s))
    )


def ring(a, s):
    return lax.ppermute(a, AXES, permutation(lambda x, c, z, y: (x, c, z - s if c else z + s, y)))


def swap(a):
    return lax.ppermute(a, AXES, permutation(lambda x, c, z, y: (x, 1 - c, z, y)))


def call(name, body, outs, ins, scalars=(), after=(), specs=None, scratch=()):
    n_out, n_in = len(outs), len(ins) + len(scalars)

    def kernel(*refs):
        used = refs[:n_in] + refs[n_in + len(after) :]
        body(*used)

    return pl.pallas_call(
        kernel,
        out_shape=outs,
        in_specs=[SMEM] * len(scalars) + (specs or [VMEM] * len(ins)) + [ANY] * len(after),
        out_specs=[VMEM] * n_out,
        scratch_shapes=list(scratch),
        name=name,
        cost_estimate=pl.CostEstimate(flops=1, bytes_accessed=1, transcendentals=0),
        compiler_params=pltpu.CompilerParams(vmem_limit_bytes=20 * MIB),
    )(*scalars, *ins, *after)


def shape(*dims, dtype=BF16):
    return jax.ShapeDtypeStruct(dims, dtype)


def up(ref, lo, hi):
    return ref[lo:hi, :].astype(F32)


def normalize_body(img_ref, txt_ref, img_unit, txt_unit, img_inv, txt_inv, raw_ref, sem):
    copies = [
        pltpu.make_async_copy(src, raw_ref.at[i], sem.at[i])
        for i, src in enumerate((img_ref, txt_ref))
    ]
    for copy in copies:
        copy.start()
    for i, (unit, inv) in enumerate(((img_unit, img_inv), (txt_unit, txt_inv))):
        copies[i].wait()
        v = raw_ref[i].astype(F32)
        r = lax.rsqrt(jnp.sum(v * v, axis=-1, keepdims=True) + EPS)
        unit[...] = (v * r).astype(BF16)
        inv[...] = r


def split3(v):
    hi = v.astype(BF16).astype(F32)
    mid = (v - hi).astype(BF16).astype(F32)
    return hi, mid, v - hi - mid


def loss_rows(total):
    hi, mid, low = split3(total)
    at = lax.broadcasted_iota(jnp.int32, total.shape, 0)
    return jnp.where(at == 0, hi, jnp.where(at == 1, mid, jnp.where(at == 2, low, 0.0))).astype(BF16)


def loss_sum(rows):
    return jnp.sum(rows.astype(F32), axis=0, keepdims=True)


def entry(img, txt, scale, bias, match=None):
    dots = lax.dot_general(img, txt, (((1,), (1,)), ((), ())), preferred_element_type=F32)
    logits = dots * scale + bias
    if match is not None:
        logits = jnp.where(match, -logits, logits)
    e = jnp.exp(logits)
    u = 1.0 + e
    inv = 1.0 / u
    softplus = jnp.log(u) + (e - (u - 1.0)) * inv
    weight = scale * (e * inv)
    if match is not None:
        weight = jnp.where(match, -weight, weight)
    return weight.astype(BF16), softplus


def fold(v):
    total = v[:, :128]
    for n in range(1, v.shape[1] // 128):
        total = total + v[:, 128 * n : 128 * (n + 1)]
    return total


def mine_body(scale_ref, bias_ref, img_ref, txt_ref, coeff_ref, loss_ref):
    weight, softplus = entry(img_ref[...], txt_ref[...], scale_ref[0], bias_ref[0])
    coeff_ref[...] = weight
    loss_ref[...] = fold(softplus)


def texts(coeffs, imgs, lo, hi):
    total = None
    for c, s in zip(coeffs, imgs):
        part = lax.dot_general(
            c[:, lo:hi], s[...], (((0,), (0,)), ((), ())), preferred_element_type=F32
        )
        total = part if total is None else total + part
    return total


def far_body(scale_ref, bias_ref, i0, i1, i2, i3, txt_ref, near_loss, c0, c1, c2, c3, keep, send, loss):
    scale, bias = scale_ref[0], bias_ref[0]
    imgs, coeffs = (i0, i1, i2, i3), (c0, c1, c2, c3)
    for k in range(4):
        total = near_loss[256 * k : 256 * (k + 1), :]
        for lo, hi in ((0, 256), (256, 384)):
            weight, softplus = entry(imgs[k][...], txt_ref[lo:hi, :], scale, bias)
            coeffs[k][:, lo:hi] = weight
            total = total + fold(softplus)
        column = jnp.broadcast_to(jnp.sum(total, axis=1, keepdims=True), (256, 128))
        loss[:, 256 * k : 256 * (k + 1)] = jnp.transpose(column)[:8, :]
    g = texts(coeffs, imgs, 0, 384)
    keep[...] = g[:192, :]
    send[...] = g[192:, :].astype(BF16)


def other_body(scale_ref, bias_ref, i0, i1, i2, i3, c0, c1, c2, c3, txt_ref, l0, l1, l2, l3, o0, o1, o2, o3, keep, send, pair, loss):
    scale, bias = scale_ref[0], bias_ref[0]
    imgs, sums, mine, other = (i0, i1, i2, i3), (l0, l1, l2, l3), (c0, c1, c2, c3), (o0, o1, o2, o3)
    for k in range(4):
        total = sums[k][...]
        for lo, hi in ((0, 256), (256, 384)):
            match = None
            if k == 0 and lo == 256:
                r = lax.broadcasted_iota(jnp.int32, (256, 128), 0)
                c = lax.broadcasted_iota(jnp.int32, (256, 128), 1)
                match = (r == c) & (r < U)
            weight, softplus = entry(imgs[k][...], txt_ref[lo:hi, :], scale, bias, match)
            other[k][:, lo:hi] = weight
            total = total + fold(softplus)
        loss[256 * k : 256 * (k + 1), :] = total
    g = texts(other, imgs, 0, 384)
    send[...] = g[:256, :].astype(BF16)
    pair[...] = g[256:, :]
    keep[...] = texts(mine, imgs, 0, 256)


def image_body(k, cf, cm, co, far, mine, other, loss, out):
    g = jnp.dot(cf[...], far[...], preferred_element_type=F32)
    g = g + jnp.dot(cm[...], mine[...], preferred_element_type=F32)
    g = g + jnp.dot(co[...], other[...], preferred_element_type=F32)
    if k == 0:
        out[...] = g
    else:
        out[:256, :] = g.astype(BF16)
        out[256:, :] = jnp.zeros((8, g.shape[1]), BF16)
        out[256:, :256] = loss_rows(loss[:, 256 * k : 256 * (k + 1)])


def merge_img_body(g_ref, l_ref, r1, r2, r3, own_ref, own_loss, m1, m2, m3):
    loss = l_ref[:, :256] + (
        loss_sum(r1[256:, :256]) + loss_sum(r2[256:, :256]) + loss_sum(r3[256:, :256])
    )
    own_loss[...] = loss
    marks = loss_rows(loss)
    for j, out in enumerate((own_ref, m1, m2, m3)):
        lo, hi = U * j, U * (j + 1)
        total = g_ref[lo:hi, :] + (up(r1, lo, hi) + up(r2, lo, hi) + up(r3, lo, hi))
        out[:U, :] = total.astype(out.dtype)
        if j:
            out[U:, :] = jnp.zeros((8, total.shape[1]), BF16)
            out[U:, :256] = marks


def pack_body(*refs):
    out, at = refs[-1], 0
    for ref in refs[:-1]:
        n = min(ref.shape[0], out.shape[0] - at)
        out[at : at + n, :] = ref[:n, :]
        at += n


def step1_body(keep, got, two, one):
    two[...] = (keep[:64, :] + up(got, 0, 64)).astype(BF16)
    one[...] = (keep[64:, :] + up(got, 64, 192)).astype(BF16)


def step2_body(keep, got, v2, v1, out):
    total = keep[:128, :] + (up(got, 0, 128) + up(v1, 0, 128))
    out[:64, :] = (total[:64, :] + up(v2, 0, 64)).astype(BF16)
    out[64:, :] = total[64:, :].astype(BF16)


def step3_body(keep, got, w, out):
    out[...] = (keep[128:, :] + (up(got, 128, 256) + up(w, 0, 128))).astype(BF16)


def step4_body(pair, w, out):
    out[...] = (pair[64:, :] + up(w, 64, 128)).astype(BF16)


def back_norm(g, raw, inv):
    unit = raw[...].astype(F32) * inv[...]
    return inv[...] * (g - unit * jnp.sum(unit * g, axis=-1, keepdims=True))


def finish_img_body(g_ref, l_ref, r1, r2, r3, raw, inv, out_ref, loss_ref, done_ref):
    done_ref[...] = l_ref[:, :128]
    g = g_ref[...] + (up(r1, 0, U) + up(r2, 0, U) + up(r3, 0, U))
    out_ref[...] = back_norm(g, raw, inv)
    loss = l_ref[:1, :U]
    for j, r in enumerate((r1, r2, r3)):
        loss = loss + loss_sum(r[U:, U * (j + 1) : U * (j + 2)])
    loss_ref[...] = loss


def finish_txt_body(pair, w, got, raw, inv, out_ref):
    g = pair[:64, :] + (up(w, 0, 64) + got[...].astype(F32))
    out_ref[...] = back_norm(g, raw, inv)


def on_device(picture, caption, scale, bias):
    rows, d = picture.shape
    img, txt, img_inv, txt_inv = call(
        "normalize", normalize_body,
        [shape(rows, d), shape(rows, d), shape(rows, 1, dtype=F32), shape(rows, 1, dtype=F32)],
        [pltpu.with_memory_space_constraint(a, pltpu.HBM) for a in (picture, caption)], specs=[HBM] * 2,
        scratch=[pltpu.VMEM((2, rows, d), BF16), pltpu.SemaphoreType.DMA((2,))],
    )

    def pack(name, n, parts, after=()):
        return call(name, pack_body, [shape(n, d)], parts, (), after)[0]

    pair = pack("pair", 128, (txt, swap(txt)))
    b1 = ring(pair, 1)
    f1, f3, f2 = first(img, 1), first(img, 3), first(img, 2)
    group = pack("group", 256, (img, f1, f2, f3))
    g1, g3, g2 = second(group, 1), second(group, 3), second(group, 2)
    groups = (group, g1, g2, g3)
    b1 = pack("behind1", 128, (b1,), (group,))
    b2, a1 = ring(b1, 1), swap(b1)
    b2 = pack("behind2", 128, (b2,), (a1,))
    b3, a2 = ring(b2, 1), swap(b2)
    far_first = pack("far_first", 64, (b3,), (a2,))
    b4 = ring(far_first, 1)
    near_mine = pack("near_mine", 256, (b2, b1), (far_first,))
    other = pack("other_texts", 384, (a2, a1, pair), (near_mine,))

    sc = (scale, bias)
    mine_c, mine_l, last = [None] * 4, [None] * 4, (other,)
    for k in (0, 1, 3, 2):
        mine_c[k], mine_l[k] = call(
            f"mine{k}", mine_body, [shape(256, 256), shape(256, 128, dtype=F32)],
            (groups[k], near_mine), sc, last,
        )
        last = (mine_l[k],)
    *other_c, keep_b, send_b, own_pair, near_loss = call(
        "other", other_body,
        [shape(256, 384)] * 4
        + [shape(256, d, dtype=F32), shape(256, d), shape(128, d, dtype=F32), shape(1024, 128, dtype=F32)],
        (*groups, *mine_c, other, *mine_l), sc, last,
    )
    got_b = swap(send_b)
    far_mine = pack("far_mine", 192, (b4, b3), (send_b,))
    far = pack("far_texts", 384, (far_mine, swap(far_mine)))
    *far_c, keep_a, send_a, loss = call(
        "far", far_body,
        [shape(256, 384)] * 4 + [shape(192, d, dtype=F32), shape(192, d), shape(8, 1024, dtype=F32)],
        (*groups, far, near_loss), sc,
    )
    got_a = swap(send_a)

    def image(k, after):
        out = shape(256, d, dtype=F32) if k == 0 else shape(264, d)
        return call(
            f"image{k}", functools.partial(image_body, k), [out],
            (far_c[k], mine_c[k], other_c[k], far, near_mine, other, loss), (), after,
        )[0]

    p1 = image(1, ())
    r1 = second(p1, -1)
    two, one = call("step1", step1_body, [shape(64, d), shape(128, d)], (keep_a, got_a), (), (p1, got_b))
    v2, v1 = ring(two, -2), ring(one, -1)
    p3 = image(3, (one,))
    r3 = second(p3, -3)
    p2 = image(2, (p3,))
    r2 = second(p2, -2)
    p0 = image(0, (p2,))
    z2 = call("step2", step2_body, [shape(128, d)], (keep_b, got_b, v2, v1), (), (p0,))[0]
    w2 = ring(z2, -1)
    own_img, own_loss, m1, m2, m3 = call(
        "merge_img", merge_img_body,
        [shape(rows, d, dtype=F32), shape(8, 256, dtype=F32)] + [shape(rows + 8, d)] * 3,
        (p0, loss, r1, r2, r3), (), (z2,),
    )
    q1, q3, q2 = first(m1, -1), first(m3, -3), first(m2, -2)
    z3 = call("step3", step3_body, [shape(128, d)], (keep_b, got_b, w2), (), (m3,))[0]
    w3 = ring(z3, -1)
    grad_img, loss_out, done = call(
        "finish_img", finish_img_body,
        [shape(rows, d, dtype=F32), shape(1, rows, dtype=F32), shape(8, 128, dtype=F32)],
        (own_img, own_loss, q1, q2, q3, picture, img_inv), (), (z3,),
    )
    z4 = call("step4", step4_body, [shape(64, d)], (own_pair, w3), (), (done,))[0]
    got_c = swap(z4)
    grad_txt = call(
        "finish_txt", finish_txt_body, [shape(rows, d, dtype=F32)],
        (own_pair, w3, got_c, caption, txt_inv),
    )[0]
    return grad_img, grad_txt, loss_out.reshape(rows)


def solution(mesh):
    torus = Mesh(mesh.devices.reshape(NX, NC, NZ, NY), AXES)
    return jax.shard_map(
        on_device,
        mesh=torus,
        in_specs=(P(AXES, None), P(AXES, None), P(), P()),
        out_specs=(P(AXES, None), P(AXES, None), P(AXES)),
        check_vma=False,
    )
```

```python
import functools

import jax
import jax.numpy as jnp
from jax import lax
from jax.experimental import pallas as pl
from jax.experimental.pallas import tpu as pltpu
from jax.sharding import Mesh
from jax.sharding import PartitionSpec as P

AXES = ("x", "core", "z", "y")
NX, NC, NZ, NY = 4, 2, 8, 4
U = 64
EPS = 1e-06
F32 = jnp.float32
BF16 = jnp.bfloat16
MIB = 1 << 20
VMEM = pl.BlockSpec(memory_space=pltpu.VMEM)
SMEM = pl.BlockSpec(memory_space=pltpu.SMEM)
ANY = pl.BlockSpec(memory_space=pl.ANY)
HBM = pl.BlockSpec(memory_space=pltpu.HBM)


def device(x, core, z, y):
    return ((x % NX * NC + core) * NZ + z % NZ) * NY + y % NY


def permutation(move):
    return [
        (device(x, c, z, y), device(*move(x, c, z, y)))
        for x in range(NX)
        for c in range(NC)
        for z in range(NZ)
        for y in range(NY)
    ]


def first(a, s):
    return lax.ppermute(
        a, AXES, permutation(lambda x, c, z, y: (x, c, z, y + s) if c else (x + s, c, z, y))
    )


def second(a, s):
    return lax.ppermute(
        a, AXES, permutation(lambda x, c, z, y: (x + s, c, z, y) if c else (x, c, z, y + s))
    )


def ring(a, s):
    return lax.ppermute(a, AXES, permutation(lambda x, c, z, y: (x, c, z - s if c else z + s, y)))


def swap(a):
    return lax.ppermute(a, AXES, permutation(lambda x, c, z, y: (x, 1 - c, z, y)))


def call(name, body, outs, ins, scalars=(), after=(), specs=None, scratch=()):
    n_out, n_in = len(outs), len(ins) + len(scalars)

    def kernel(*refs):
        used = refs[:n_in] + refs[n_in + len(after) :]
        body(*used)

    return pl.pallas_call(
        kernel,
        out_shape=outs,
        in_specs=[SMEM] * len(scalars) + (specs or [VMEM] * len(ins)) + [ANY] * len(after),
        out_specs=[VMEM] * n_out,
        scratch_shapes=list(scratch),
        name=name,
        cost_estimate=pl.CostEstimate(flops=1, bytes_accessed=1, transcendentals=0),
        compiler_params=pltpu.CompilerParams(vmem_limit_bytes=20 * MIB),
    )(*scalars, *ins, *after)


def shape(*dims, dtype=BF16):
    return jax.ShapeDtypeStruct(dims, dtype)


def up(ref, lo, hi):
    return ref[lo:hi, :].astype(F32)


def normalize_body(img_ref, txt_ref, img_unit, txt_unit, img_inv, txt_inv, raw_ref, sem):
    copies = [
        pltpu.make_async_copy(src, raw_ref.at[i], sem.at[i])
        for i, src in enumerate((img_ref, txt_ref))
    ]
    for copy in copies:
        copy.start()
    for i, (unit, inv) in enumerate(((img_unit, img_inv), (txt_unit, txt_inv))):
        copies[i].wait()
        v = raw_ref[i].astype(F32)
        r = lax.rsqrt(jnp.sum(v * v, axis=-1, keepdims=True) + EPS)
        unit[...] = (v * r).astype(BF16)
        inv[...] = r


def split3(v):
    hi = v.astype(BF16).astype(F32)
    mid = (v - hi).astype(BF16).astype(F32)
    return hi, mid, v - hi - mid


def loss_rows(total):
    hi, mid, low = split3(total)
    at = lax.broadcasted_iota(jnp.int32, total.shape, 0)
    return jnp.where(at == 0, hi, jnp.where(at == 1, mid, jnp.where(at == 2, low, 0.0))).astype(BF16)


def loss_sum(rows):
    return jnp.sum(rows.astype(F32), axis=0, keepdims=True)


def entry(img, txt, scale, bias, match=None):
    dots = lax.dot_general(img, txt, (((1,), (1,)), ((), ())), preferred_element_type=F32)
    logits = dots * scale + bias
    if match is not None:
        logits = jnp.where(match, -logits, logits)
    e = jnp.exp(logits)
    u = 1.0 + e
    inv = 1.0 / u
    softplus = jnp.log(u) + (e - (u - 1.0)) * inv
    weight = scale * (e * inv)
    if match is not None:
        weight = jnp.where(match, -weight, weight)
    return weight.astype(BF16), softplus


def fold(v):
    total = v[:, :128]
    for n in range(1, v.shape[1] // 128):
        total = total + v[:, 128 * n : 128 * (n + 1)]
    return total


def mine_body(scale_ref, bias_ref, img_ref, txt_ref, coeff_ref, loss_ref):
    weight, softplus = entry(img_ref[:256, :], txt_ref[...], scale_ref[0], bias_ref[0])
    coeff_ref[...] = weight
    loss_ref[...] = fold(softplus)


def texts(coeffs, imgs, lo, hi):
    total = None
    for c, s in zip(coeffs, imgs):
        part = lax.dot_general(
            c[:, lo:hi], s[:256, :], (((0,), (0,)), ((), ())), preferred_element_type=F32
        )
        total = part if total is None else total + part
    return total


def tile(img, txt_ref, coeff_ref, total, scale, bias, own=False):
    for lo, hi in ((0, 256), (256, 384)):
        match = None
        if own and lo == 256:
            r = lax.broadcasted_iota(jnp.int32, (256, 128), 0)
            c = lax.broadcasted_iota(jnp.int32, (256, 128), 1)
            match = (r == c) & (r < U)
        weight, softplus = entry(img[:256, :], txt_ref[lo:hi, :], scale, bias, match)
        coeff_ref[:, lo:hi] = weight
        total = total + fold(softplus)
    return total


def other_body(scale_ref, bias_ref, i0, i1, i3, txt_ref, l0, l1, l3, o0, o1, o3, loss):
    for n, (i, o, l) in enumerate(((i0, o0, l0), (i1, o1, l1), (i3, o3, l3))):
        loss[256 * n : 256 * (n + 1), :] = tile(
            i, txt_ref, o, l[...], scale_ref[0], bias_ref[0], n == 0
        )


def last_body(scale_ref, bias_ref, i0, i1, i2, i3, near, other, m0, m1, m3, o0, o1, o3, m2, o2, loss, keep, send, pair):
    scale, bias = scale_ref[0], bias_ref[0]
    imgs = (i0, i1, i2, i3)
    weight, softplus = entry(i2[:256, :], near[...], scale, bias)
    m2[...] = weight
    loss[...] = tile(i2, other, o2, fold(softplus), scale, bias)
    g = texts((o0, o1, o2, o3), imgs, 0, 384)
    send[...] = g[:256, :].astype(BF16)
    pair[...] = g[256:, :]
    keep[...] = texts((m0, m1, m2, m3), imgs, 0, 256)


def far_body(scale_ref, bias_ref, i0, i1, i2, i3, txt_ref, l013, l2, c0, c1, c2, c3, keep, send, loss):
    imgs, coeffs = (i0, i1, i2, i3), (c0, c1, c2, c3)
    before = (l013[:256, :], l013[256:512, :], l2[...], l013[512:, :])
    for k in range(4):
        total = tile(imgs[k], txt_ref, coeffs[k], before[k], scale_ref[0], bias_ref[0])
        column = jnp.broadcast_to(jnp.sum(total, axis=1, keepdims=True), (256, 128))
        loss[:, 256 * k : 256 * (k + 1)] = jnp.transpose(column)[:8, :]
    g = texts(coeffs, imgs, 0, 384)
    keep[...] = g[:192, :]
    send[...] = g[192:, :].astype(BF16)


def image_body(k, cf, cm, co, far, mine, other, loss, out):
    g = jnp.dot(cf[...], far[...], preferred_element_type=F32)
    g = g + jnp.dot(cm[...], mine[...], preferred_element_type=F32)
    g = g + jnp.dot(co[...], other[...], preferred_element_type=F32)
    if k == 0:
        out[...] = g
    else:
        out[:256, :] = g.astype(BF16)
        out[256:, :] = jnp.zeros((8, g.shape[1]), BF16)
        out[256:, :256] = loss_rows(loss[:, 256 * k : 256 * (k + 1)])


def merge_img_body(g_ref, l_ref, r1, r2, r3, own_ref, own_loss, m1, m2, m3):
    loss = l_ref[:, :256] + (
        loss_sum(r1[256:, :256]) + loss_sum(r2[256:, :256]) + loss_sum(r3[256:, :256])
    )
    own_loss[...] = loss
    marks = loss_rows(loss)
    for j, out in enumerate((own_ref, m1, m2, m3)):
        lo, hi = U * j, U * (j + 1)
        total = g_ref[lo:hi, :] + (up(r1, lo, hi) + up(r2, lo, hi) + up(r3, lo, hi))
        out[:U, :] = total.astype(out.dtype)
        if j:
            out[U:, :] = jnp.zeros((8, total.shape[1]), BF16)
            out[U:, :256] = marks


def pack_body(*refs):
    out, at = refs[-1], 0
    for ref in refs[:-1]:
        n = min(ref.shape[0], out.shape[0] - at)
        out[at : at + n, :] = ref[:n, :]
        at += n
    if at < out.shape[0]:
        out[at:, :] = jnp.zeros((out.shape[0] - at, out.shape[1]), out.dtype)


def split_body(b1, b2, far, near):
    far[:U, :] = b2[:U, :]
    far[U:, :] = b1[...]
    near[:128, :] = b2[...]
    near[128:, :] = b1[...]


def step1_body(keep, got, out):
    out[...] = (keep[...] + got[...].astype(F32)).astype(BF16)


def step2_body(keep, got, w, two, one):
    two[:64, :] = (keep[:64, :] + (up(got, 0, 64) + up(w, 0, 64))).astype(BF16)
    two[64:, :] = (keep[64:128, :] + up(got, 64, 128)).astype(BF16)
    one[...] = (keep[128:, :] + (up(got, 128, 256) + up(w, 64, 192))).astype(BF16)


def step3_body(pair, v1, v2, out):
    out[...] = (pair[64:, :] + (up(v1, 64, 128) + up(v2, 64, 128))).astype(BF16)


def back_norm(g, raw, inv):
    unit = raw[...].astype(F32) * inv[...]
    return inv[...] * (g - unit * jnp.sum(unit * g, axis=-1, keepdims=True))


def finish_body(g_ref, l_ref, r1, r2, r3, raw_i, inv_i, pair, v1, v2, got, raw_t, inv_t, img_ref, txt_ref, loss_ref):
    g = g_ref[...] + (up(r1, 0, U) + up(r2, 0, U) + up(r3, 0, U))
    img_ref[...] = back_norm(g, raw_i, inv_i)
    loss = l_ref[:1, :U]
    for j, r in enumerate((r1, r2, r3)):
        loss = loss + loss_sum(r[U:, U * (j + 1) : U * (j + 2)])
    loss_ref[...] = loss
    g = pair[:64, :] + (up(v1, 0, 64) + up(v2, 0, 64) + got[...].astype(F32))
    txt_ref[...] = back_norm(g, raw_t, inv_t)


def on_device(picture, caption, scale, bias):
    rows, d = picture.shape
    img, txt, img_inv, txt_inv = call(
        "normalize", normalize_body,
        [shape(rows, d), shape(rows, d), shape(rows, 1, dtype=F32), shape(rows, 1, dtype=F32)],
        [pltpu.with_memory_space_constraint(a, pltpu.HBM) for a in (picture, caption)], specs=[HBM] * 2,
        scratch=[pltpu.VMEM((2, rows, d), BF16), pltpu.SemaphoreType.DMA((2,))],
    )

    def pack(name, n, parts, after=()):
        return call(name, pack_body, [shape(n, d)], parts, (), after)[0]

    pair = pack("pair", 128, (txt, swap(txt)))
    b2, b1 = ring(pair, 2), ring(pair, 1)
    f2, f1, f3 = first(img, 2), first(img, 1), first(img, 3)
    group = pack("group", 264, (img, f1, f2, f3))
    g1, g3, g2 = second(group, 1), second(group, 3), second(group, 2)
    groups = (group, g1, g2, g3)
    far_pack, near_mine = call(
        "pack", split_body, [shape(192, d), shape(256, d)], (b1, b2), (), (group,)
    )
    far_got = ring(far_pack, 2)
    near_other = swap(near_mine)

    sc = (scale, bias)
    mine_c, mine_l, other_c, last = [None] * 4, [None] * 4, [None] * 4, ()
    for k in (0, 1, 3):
        mine_c[k], mine_l[k] = call(
            f"mine{k}", mine_body, [shape(256, 256), shape(256, 128, dtype=F32)],
            (groups[k], near_mine), sc, last,
        )
        last = (mine_l[k],)
    other = pack("other_texts", 384, (near_other, pair), last)
    other_c[0], other_c[1], other_c[3], near_loss = call(
        "other", other_body, [shape(256, 384)] * 3 + [shape(768, 128, dtype=F32)],
        (groups[0], groups[1], groups[3], other, mine_l[0], mine_l[1], mine_l[3]), sc,
    )
    mine_c[2], other_c[2], last_loss, keep_b, send_b, own_pair = call(
        "last", last_body,
        [shape(256, 256), shape(256, 384), shape(256, 128, dtype=F32)]
        + [shape(256, d, dtype=F32), shape(256, d), shape(128, d, dtype=F32)],
        (*groups, near_mine, other, mine_c[0], mine_c[1], mine_c[3], other_c[0], other_c[1], other_c[3]),
        sc, (near_loss,),
    )
    got_b = swap(send_b)
    far_mine = pack("far_mine", 192, (far_got,), (send_b,))
    far = pack("far_texts", 384, (far_mine, swap(far_mine)))
    *far_c, keep_a, send_a, loss = call(
        "far", far_body,
        [shape(256, 384)] * 4 + [shape(192, d, dtype=F32), shape(192, d), shape(8, 1024, dtype=F32)],
        (*groups, far, near_loss, last_loss), sc,
    )
    got_a = swap(send_a)

    def image(k, after):
        out = shape(256, d, dtype=F32) if k == 0 else shape(264, d)
        return call(
            f"image{k}", functools.partial(image_body, k), [out],
            (far_c[k], mine_c[k], other_c[k], far, near_mine, other, loss), (), after,
        )[0]

    p1 = image(1, ())
    r1 = second(p1, -1)
    z1 = call("step1", step1_body, [shape(192, d)], (keep_a, got_a), (), (p1, got_b))[0]
    w = ring(z1, -2)
    p3 = image(3, (z1,))
    r3 = second(p3, -3)
    p2 = image(2, (p3,))
    r2 = second(p2, -2)
    p0 = image(0, (p2,))
    two, one = call("step2", step2_body, [shape(128, d)] * 2, (keep_b, got_b, w), (), (p0,))
    v2, v1 = ring(two, -2), ring(one, -1)
    own_img, own_loss, m1, m2, m3 = call(
        "merge_img", merge_img_body,
        [shape(rows, d, dtype=F32), shape(8, 256, dtype=F32)] + [shape(rows + 8, d)] * 3,
        (p0, loss, r1, r2, r3), (), (one,),
    )
    q1, q3, q2 = first(m1, -1), first(m3, -3), first(m2, -2)
    z3 = call("step3", step3_body, [shape(64, d)], (own_pair, v1, v2), (), (m3,))[0]
    got_c = swap(z3)
    grad_img, grad_txt, loss_out = call(
        "finish", finish_body,
        [shape(rows, d, dtype=F32), shape(rows, d, dtype=F32), shape(1, rows, dtype=F32)],
        (own_img, own_loss, q1, q2, q3, picture, img_inv, own_pair, v1, v2, got_c, caption, txt_inv),
    )
    return grad_img, grad_txt, loss_out.reshape(rows)


def solution(mesh):
    torus = Mesh(mesh.devices.reshape(NX, NC, NZ, NY), AXES)
    return jax.shard_map(
        on_device,
        mesh=torus,
        in_specs=(P(AXES, None), P(AXES, None), P(), P()),
        out_specs=(P(AXES, None), P(AXES, None), P(AXES)),
        check_vma=False,
    )
```

```python
import functools

import jax
import jax.numpy as jnp
from jax import lax
from jax.experimental import pallas as pl
from jax.experimental.pallas import tpu as pltpu
from jax.sharding import Mesh
from jax.sharding import PartitionSpec as P

AXES = ("x", "core", "z", "y")
NX, NC, NZ, NY = 4, 2, 8, 4
U = 64
EPS = 1e-06
F32 = jnp.float32
BF16 = jnp.bfloat16
MIB = 1 << 20
VMEM = pl.BlockSpec(memory_space=pltpu.VMEM)
SMEM = pl.BlockSpec(memory_space=pltpu.SMEM)
ANY = pl.BlockSpec(memory_space=pl.ANY)
HBM = pl.BlockSpec(memory_space=pltpu.HBM)


def device(x, core, z, y):
    return ((x % NX * NC + core) * NZ + z % NZ) * NY + y % NY


def permutation(move):
    return [
        (device(x, c, z, y), device(*move(x, c, z, y)))
        for x in range(NX)
        for c in range(NC)
        for z in range(NZ)
        for y in range(NY)
    ]


def first(a, s):
    return lax.ppermute(
        a, AXES, permutation(lambda x, c, z, y: (x, c, z, y + s) if c else (x + s, c, z, y))
    )


def second(a, s):
    return lax.ppermute(
        a, AXES, permutation(lambda x, c, z, y: (x + s, c, z, y) if c else (x, c, z, y + s))
    )


def ring(a, s):
    return lax.ppermute(a, AXES, permutation(lambda x, c, z, y: (x, c, z - s if c else z + s, y)))


def swap(a):
    return lax.ppermute(a, AXES, permutation(lambda x, c, z, y: (x, 1 - c, z, y)))


def call(name, body, outs, ins, scalars=(), after=(), specs=None, scratch=()):
    n_out, n_in = len(outs), len(ins) + len(scalars)

    def kernel(*refs):
        used = refs[:n_in] + refs[n_in + len(after) :]
        body(*used)

    return pl.pallas_call(
        kernel,
        out_shape=outs,
        in_specs=[SMEM] * len(scalars) + (specs or [VMEM] * len(ins)) + [ANY] * len(after),
        out_specs=[VMEM] * n_out,
        scratch_shapes=list(scratch),
        name=name,
        cost_estimate=pl.CostEstimate(flops=1, bytes_accessed=1, transcendentals=0),
        compiler_params=pltpu.CompilerParams(vmem_limit_bytes=20 * MIB),
    )(*scalars, *ins, *after)


def shape(*dims, dtype=BF16):
    return jax.ShapeDtypeStruct(dims, dtype)


def up(ref, lo, hi):
    return ref[lo:hi, :].astype(F32)


def normalize_body(img_ref, txt_ref, img_unit, txt_unit, img_inv, txt_inv, raw_ref, sem):
    copies = [
        pltpu.make_async_copy(src, raw_ref.at[i], sem.at[i])
        for i, src in enumerate((img_ref, txt_ref))
    ]
    for copy in copies:
        copy.start()
    for i, (unit, inv) in enumerate(((img_unit, img_inv), (txt_unit, txt_inv))):
        copies[i].wait()
        v = raw_ref[i].astype(F32)
        r = lax.rsqrt(jnp.sum(v * v, axis=-1, keepdims=True) + EPS)
        unit[...] = (v * r).astype(BF16)
        inv[...] = r


def split3(v):
    hi = v.astype(BF16).astype(F32)
    mid = (v - hi).astype(BF16).astype(F32)
    return hi, mid, v - hi - mid


def loss_rows(total):
    hi, mid, low = split3(total)
    at = lax.broadcasted_iota(jnp.int32, total.shape, 0)
    return jnp.where(at == 0, hi, jnp.where(at == 1, mid, jnp.where(at == 2, low, 0.0))).astype(BF16)


def loss_sum(rows):
    return jnp.sum(rows.astype(F32), axis=0, keepdims=True)


def entry(img, txt, scale, bias, match=None):
    dots = lax.dot_general(img, txt, (((1,), (1,)), ((), ())), preferred_element_type=F32)
    logits = dots * scale + bias
    if match is not None:
        logits = jnp.where(match, -logits, logits)
    e = jnp.exp(logits)
    u = 1.0 + e
    inv = 1.0 / u
    softplus = jnp.log(u) + (e - (u - 1.0)) * inv
    weight = scale * (e * inv)
    if match is not None:
        weight = jnp.where(match, -weight, weight)
    return weight.astype(BF16), softplus


def fold(v):
    total = v[:, :128]
    for n in range(1, v.shape[1] // 128):
        total = total + v[:, 128 * n : 128 * (n + 1)]
    return total


def texts(coeffs, imgs, lo, hi):
    total = None
    for c, s in zip(coeffs, imgs):
        part = lax.dot_general(
            c[:, lo:hi], s[:256, :], (((0,), (0,)), ((), ())), preferred_element_type=F32
        )
        total = part if total is None else total + part
    return total


def tile(img, txt_ref, coeff_ref, total, scale, bias, own=False):
    for lo, hi in ((0, 256), (256, 384)):
        match = None
        if own and lo == 256:
            r = lax.broadcasted_iota(jnp.int32, (256, 128), 0)
            c = lax.broadcasted_iota(jnp.int32, (256, 128), 1)
            match = (r == c) & (r < U)
        weight, softplus = entry(img[:256, :], txt_ref[lo:hi, :], scale, bias, match)
        coeff_ref[:, lo:hi] = weight
        total = total + fold(softplus)
    return total


def near_tile(img, mine_ref, other_ref, coeff_ref, total, scale, bias, own=False):
    weight, softplus = entry(img[:256, :], mine_ref[...], scale, bias)
    coeff_ref[:, :256] = weight
    total = total + fold(softplus)
    return tile(img, other_ref, coeff_ref.at[:, 256:], total, scale, bias, own)


def near_body(own, scale_ref, bias_ref, img, mine, other, coeff, loss):
    zero = jnp.zeros((256, 128), F32)
    loss[...] = near_tile(img, mine, other, coeff, zero, scale_ref[0], bias_ref[0], own)


def loss_row(total):
    column = jnp.broadcast_to(jnp.sum(total, axis=1, keepdims=True), (256, 128))
    return jnp.transpose(column)[:8, :]


def image(cn, cf, mine, other, far):
    g = jnp.dot(cf[...], far[...], preferred_element_type=F32)
    g = g + jnp.dot(cn[:, :256], mine[...], preferred_element_type=F32)
    return g + jnp.dot(cn[:, 256:], other[...], preferred_element_type=F32)


def send_image(out, g, loss):
    out[:256, :] = g.astype(BF16)
    out[256:, :] = jnp.zeros((8, g.shape[1]), BF16)
    out[256:, :256] = loss_rows(loss)


def far_image_body(scale_ref, bias_ref, img, mine, other, far, cn, loss, cf, out):
    total = tile(img, far, cf, loss[...], scale_ref[0], bias_ref[0])
    send_image(out, image(cn, cf, mine, other, far), loss_row(total))


def far_own_body(scale_ref, bias_ref, img, far, loss, cf, row):
    row[...] = loss_row(tile(img, far, cf, loss[...], scale_ref[0], bias_ref[0]))


def last_body(scale_ref, bias_ref, img, mine, other, far, cn, cf, row):
    scale, bias = scale_ref[0], bias_ref[0]
    total = near_tile(img, mine, other, cn, jnp.zeros((256, 128), F32), scale, bias)
    row[...] = loss_row(tile(img, far, cf, total, scale, bias))


def near_part_body(c0, c1, c3, i0, i1, i3, part):
    part[...] = texts((c0, c1, c3), (i0, i1, i3), 0, 640)


def texts_body(c0, c1, c2, c3, n2, i0, i1, i2, i3, part, keep_a, send_a, keep_b, send_b, pair):
    g = texts((c0, c1, c2, c3), (i0, i1, i2, i3), 0, 384)
    keep_a[...] = g[:192, :]
    send_a[...] = g[192:, :].astype(BF16)
    g = part[...] + texts((n2,), (i2,), 0, 640)
    keep_b[...] = g[:256, :]
    send_b[...] = g[256:512, :].astype(BF16)
    pair[...] = g[512:, :]


def last_image_body(cn, cf, mine, other, far, row, out):
    send_image(out, image(cn, cf, mine, other, far), row[...])


def own_image_body(cn, cf, mine, other, far, row, r1, r3, out, loss):
    out[...] = image(cn, cf, mine, other, far) + (up(r1, 0, 256) + up(r3, 0, 256))
    loss[...] = row[...] + (loss_sum(r1[256:, :256]) + loss_sum(r3[256:, :256]))


def merge_img_body(g_ref, l_ref, r2, own_ref, own_loss, m1, m2, m3):
    loss = l_ref[...] + loss_sum(r2[256:, :256])
    own_loss[...] = loss
    marks = loss_rows(loss)
    for j, out in enumerate((own_ref, m1, m2, m3)):
        lo, hi = U * j, U * (j + 1)
        total = g_ref[lo:hi, :] + up(r2, lo, hi)
        out[:U, :] = total.astype(out.dtype)
        if j:
            out[U:, :] = jnp.zeros((8, total.shape[1]), BF16)
            out[U:, :256] = marks


def pack_body(*refs):
    out, at = refs[-1], 0
    for ref in refs[:-1]:
        n = min(ref.shape[0], out.shape[0] - at)
        out[at : at + n, :] = ref[:n, :]
        at += n
    if at < out.shape[0]:
        out[at:, :] = jnp.zeros((out.shape[0] - at, out.shape[1]), out.dtype)


def split_body(b1, b2, far, near):
    far[:U, :] = b2[:U, :]
    far[U:, :] = b1[...]
    near[:128, :] = b2[...]
    near[128:, :] = b1[...]


def step1_body(keep, got, out):
    out[...] = (keep[...] + got[...].astype(F32)).astype(BF16)


def step2_body(keep, got, w, two, one):
    two[:64, :] = (keep[:64, :] + (up(got, 0, 64) + up(w, 0, 64))).astype(BF16)
    two[64:, :] = (keep[64:128, :] + up(got, 64, 128)).astype(BF16)
    one[...] = (keep[128:, :] + (up(got, 128, 256) + up(w, 64, 192))).astype(BF16)


def step3_body(pair, v1, v2, out):
    out[...] = (pair[64:, :] + (up(v1, 64, 128) + up(v2, 64, 128))).astype(BF16)


def back_norm(g, raw, inv):
    unit = raw[...].astype(F32) * inv[...]
    return inv[...] * (g - unit * jnp.sum(unit * g, axis=-1, keepdims=True))


def finish_body(g_ref, l_ref, r1, r2, r3, raw_i, inv_i, pair, v1, v2, got, raw_t, inv_t, img_ref, txt_ref, loss_ref):
    g = g_ref[...] + (up(r1, 0, U) + up(r2, 0, U) + up(r3, 0, U))
    img_ref[...] = back_norm(g, raw_i, inv_i)
    loss = l_ref[:1, :U]
    for j, r in enumerate((r1, r2, r3)):
        loss = loss + loss_sum(r[U:, U * (j + 1) : U * (j + 2)])
    loss_ref[...] = loss
    g = pair[:64, :] + (up(v1, 0, 64) + up(v2, 0, 64) + got[...].astype(F32))
    txt_ref[...] = back_norm(g, raw_t, inv_t)


def on_device(picture, caption, scale, bias):
    rows, d = picture.shape
    img, txt, img_inv, txt_inv = call(
        "normalize", normalize_body,
        [shape(rows, d), shape(rows, d), shape(rows, 1, dtype=F32), shape(rows, 1, dtype=F32)],
        [pltpu.with_memory_space_constraint(a, pltpu.HBM) for a in (picture, caption)], specs=[HBM] * 2,
        scratch=[pltpu.VMEM((2, rows, d), BF16), pltpu.SemaphoreType.DMA((2,))],
    )

    def pack(name, n, parts, after=()):
        return call(name, pack_body, [shape(n, d)], parts, (), after)[0]

    pair = pack("pair", 128, (txt, swap(txt)))
    b2, b1 = ring(pair, 2), ring(pair, 1)
    f2, f1, f3 = first(img, 2), first(img, 1), first(img, 3)
    group = pack("group", 264, (img, f1, f2, f3))
    g1, g3, g2 = second(group, 1), second(group, 3), second(group, 2)
    groups = (group, g1, g2, g3)
    far_pack, near_mine = call(
        "pack", split_body, [shape(192, d), shape(256, d)], (b1, b2), (), (group,)
    )
    far_got = ring(far_pack, 2)
    near_other = swap(near_mine)

    sc = (scale, bias)
    other = pack("other_texts", 384, (near_other, pair))
    near_c, near_l, last = [None] * 4, [None] * 4, ()
    for k in (0, 1, 3):
        near_c[k], near_l[k] = call(
            f"near{k}", functools.partial(near_body, k == 0), [shape(256, 640), shape(256, 128, dtype=F32)],
            (groups[k], near_mine, other), sc, last,
        )
        last = (near_l[k],)
    part = call(
        "near_part", near_part_body, [shape(640, d, dtype=F32)],
        (near_c[0], near_c[1], near_c[3], groups[0], groups[1], groups[3]), (), last,
    )[0]
    far_mine = pack("far_mine", 192, (far_got,), (part,))
    far = pack("far_texts", 384, (far_mine, swap(far_mine)))
    far_c, sent, last = [None] * 4, [None] * 4, ()
    for k in (1, 3):
        far_c[k], sent[k] = call(
            f"far_image{k}", far_image_body, [shape(256, 384), shape(264, d)],
            (groups[k], near_mine, other, far, near_c[k], near_l[k]), sc, last,
        )
        last = (sent[k],)
    r1, r3 = second(sent[1], -1), second(sent[3], -3)
    far_c[0], row0 = call(
        "far_own", far_own_body, [shape(256, 384), shape(8, 256, dtype=F32)],
        (groups[0], far, near_l[0]), sc, last,
    )
    near_c[2], far_c[2], row2 = call(
        "last", last_body, [shape(256, 640), shape(256, 384), shape(8, 256, dtype=F32)],
        (groups[2], near_mine, other, far), sc, (row0,),
    )
    keep_a, send_a, keep_b, send_b, own_pair = call(
        "texts_grad", texts_body,
        [shape(192, d, dtype=F32), shape(192, d), shape(256, d, dtype=F32), shape(256, d), shape(128, d, dtype=F32)],
        (*far_c, near_c[2], *groups, part),
    )
    got_a = swap(send_a)
    sent[2] = call(
        "last_image", last_image_body, [shape(264, d)],
        (near_c[2], far_c[2], near_mine, other, far, row2), (), (send_a,),
    )[0]
    r2 = second(sent[2], -2)

    z1 = call("step1", step1_body, [shape(192, d)], (keep_a, got_a), (), (sent[2],))[0]
    w = ring(z1, -2)
    got_b = swap(send_b)
    p0, loss = call(
        "own_image", own_image_body, [shape(256, d, dtype=F32), shape(8, 256, dtype=F32)],
        (near_c[0], far_c[0], near_mine, other, far, row0, r1, r3), (), (z1,),
    )
    two, one = call("step2", step2_body, [shape(128, d)] * 2, (keep_b, got_b, w), (), (p0,))
    v2, v1 = ring(two, -2), ring(one, -1)
    own_img, own_loss, m1, m2, m3 = call(
        "merge_img", merge_img_body,
        [shape(rows, d, dtype=F32), shape(8, 256, dtype=F32)] + [shape(rows + 8, d)] * 3,
        (p0, loss, r2), (), (one,),
    )
    q1, q3, q2 = first(m1, -1), first(m3, -3), first(m2, -2)
    z3 = call("step3", step3_body, [shape(64, d)], (own_pair, v1, v2), (), (m3,))[0]
    got_c = swap(z3)
    grad_img, grad_txt, loss_out = call(
        "finish", finish_body,
        [shape(rows, d, dtype=F32), shape(rows, d, dtype=F32), shape(1, rows, dtype=F32)],
        (own_img, own_loss, q1, q2, q3, picture, img_inv, own_pair, v1, v2, got_c, caption, txt_inv),
    )
    return grad_img, grad_txt, loss_out.reshape(rows)


def solution(mesh):
    torus = Mesh(mesh.devices.reshape(NX, NC, NZ, NY), AXES)
    return jax.shard_map(
        on_device,
        mesh=torus,
        in_specs=(P(AXES, None), P(AXES, None), P(), P()),
        out_specs=(P(AXES, None), P(AXES, None), P(AXES)),
        check_vma=False,
    )
```

```python
import functools

import jax
import jax.numpy as jnp
from jax import lax
from jax.experimental import pallas as pl
from jax.experimental.pallas import tpu as pltpu
from jax.sharding import Mesh
from jax.sharding import PartitionSpec as P

AXES = ("x", "core", "z", "y")
NX, NC, NZ, NY = 4, 2, 8, 4
U = 64
EPS = 1e-06
F32 = jnp.float32
BF16 = jnp.bfloat16
MIB = 1 << 20
VMEM = pl.BlockSpec(memory_space=pltpu.VMEM)
SMEM = pl.BlockSpec(memory_space=pltpu.SMEM)
ANY = pl.BlockSpec(memory_space=pl.ANY)
HBM = pl.BlockSpec(memory_space=pltpu.HBM)


def device(x, core, z, y):
    return ((x % NX * NC + core) * NZ + z % NZ) * NY + y % NY


def permutation(move):
    return [
        (device(x, c, z, y), device(*move(x, c, z, y)))
        for x in range(NX)
        for c in range(NC)
        for z in range(NZ)
        for y in range(NY)
    ]


def first(a, s):
    return lax.ppermute(
        a, AXES, permutation(lambda x, c, z, y: (x, c, z, y + s) if c else (x + s, c, z, y))
    )


def second(a, s):
    return lax.ppermute(
        a, AXES, permutation(lambda x, c, z, y: (x + s, c, z, y) if c else (x, c, z, y + s))
    )


def ring(a, s):
    return lax.ppermute(a, AXES, permutation(lambda x, c, z, y: (x, c, z - s if c else z + s, y)))


def swap(a):
    return lax.ppermute(a, AXES, permutation(lambda x, c, z, y: (x, 1 - c, z, y)))


def call(name, body, outs, ins, scalars=(), after=(), specs=None, scratch=()):
    n_out, n_in = len(outs), len(ins) + len(scalars)

    def kernel(*refs):
        used = refs[:n_in] + refs[n_in + len(after) :]
        body(*used)

    return pl.pallas_call(
        kernel,
        out_shape=outs,
        in_specs=[SMEM] * len(scalars) + (specs or [VMEM] * len(ins)) + [ANY] * len(after),
        out_specs=[VMEM] * n_out,
        scratch_shapes=list(scratch),
        name=name,
        cost_estimate=pl.CostEstimate(flops=1, bytes_accessed=1, transcendentals=0),
        compiler_params=pltpu.CompilerParams(vmem_limit_bytes=20 * MIB),
    )(*scalars, *ins, *after)


def shape(*dims, dtype=BF16):
    return jax.ShapeDtypeStruct(dims, dtype)


def up(ref, lo, hi):
    return ref[lo:hi, :].astype(F32)


def normalize_body(img_ref, txt_ref, img_unit, txt_unit, img_inv, txt_inv, raw_ref, sem):
    copies = [
        pltpu.make_async_copy(src, raw_ref.at[i], sem.at[i])
        for i, src in enumerate((img_ref, txt_ref))
    ]
    for copy in copies:
        copy.start()
    for i, (unit, inv) in enumerate(((img_unit, img_inv), (txt_unit, txt_inv))):
        copies[i].wait()
        v = raw_ref[i].astype(F32)
        r = lax.rsqrt(jnp.sum(v * v, axis=-1, keepdims=True) + EPS)
        unit[...] = (v * r).astype(BF16)
        inv[...] = r


def split3(v):
    hi = v.astype(BF16).astype(F32)
    mid = (v - hi).astype(BF16).astype(F32)
    return hi, mid, v - hi - mid


def loss_rows(total):
    hi, mid, low = split3(total)
    at = lax.broadcasted_iota(jnp.int32, total.shape, 0)
    return jnp.where(at == 0, hi, jnp.where(at == 1, mid, jnp.where(at == 2, low, 0.0))).astype(BF16)


def loss_sum(rows):
    return jnp.sum(rows.astype(F32), axis=0, keepdims=True)


def entry(img, txt, scale, bias, match=None):
    dots = lax.dot_general(img, txt, (((1,), (1,)), ((), ())), preferred_element_type=F32)
    logits = dots * scale + bias
    if match is not None:
        logits = jnp.where(match, -logits, logits)
    e = jnp.exp(logits)
    u = 1.0 + e
    inv = 1.0 / u
    softplus = jnp.log(u) + (e - (u - 1.0)) * inv
    weight = scale * (e * inv)
    if match is not None:
        weight = jnp.where(match, -weight, weight)
    return weight.astype(BF16), softplus


def fold(v):
    total = v[:, :128]
    for n in range(1, v.shape[1] // 128):
        total = total + v[:, 128 * n : 128 * (n + 1)]
    return total


def texts(coeffs, imgs, lo, hi):
    total = None
    for c, s in zip(coeffs, imgs):
        part = lax.dot_general(
            c[:, lo:hi], s[:256, :], (((0,), (0,)), ((), ())), preferred_element_type=F32
        )
        total = part if total is None else total + part
    return total


def tile(img, txt_ref, coeff_ref, total, scale, bias, own=False):
    for lo, hi in ((0, 256), (256, 384)):
        match = None
        if own and lo == 256:
            r = lax.broadcasted_iota(jnp.int32, (256, 128), 0)
            c = lax.broadcasted_iota(jnp.int32, (256, 128), 1)
            match = (r == c) & (r < U)
        weight, softplus = entry(img[:256, :], txt_ref[lo:hi, :], scale, bias, match)
        coeff_ref[:, lo:hi] = weight
        total = total + fold(softplus)
    return total


def near_tile(img, mine_ref, other_ref, coeff_ref, total, scale, bias, own=False):
    weight, softplus = entry(img[:256, :], mine_ref[...], scale, bias)
    coeff_ref[:, :256] = weight
    total = total + fold(softplus)
    return tile(img, other_ref, coeff_ref.at[:, 256:], total, scale, bias, own)


def near_body(own, scale_ref, bias_ref, img, mine, other, coeff, loss):
    zero = jnp.zeros((256, 128), F32)
    loss[...] = near_tile(img, mine, other, coeff, zero, scale_ref[0], bias_ref[0], own)


def loss_row(total):
    column = jnp.broadcast_to(jnp.sum(total, axis=1, keepdims=True), (256, 128))
    return jnp.transpose(column)[:8, :]


def image(cn, cf, mine, other, far):
    g = jnp.dot(cf[...], far[...], preferred_element_type=F32)
    g = g + jnp.dot(cn[:, :256], mine[...], preferred_element_type=F32)
    return g + jnp.dot(cn[:, 256:], other[...], preferred_element_type=F32)


def send_image(out, g, loss):
    out[:256, :] = g.astype(BF16)
    out[256:, :] = jnp.zeros((8, g.shape[1]), BF16)
    out[256:, :256] = loss_rows(loss)


def far_image_body(scale_ref, bias_ref, img, mine, other, far, cn, loss, cf, out):
    total = tile(img, far, cf, loss[...], scale_ref[0], bias_ref[0])
    send_image(out, image(cn, cf, mine, other, far), loss_row(total))


def far_own_body(scale_ref, bias_ref, img, far, loss, cf, row):
    row[...] = loss_row(tile(img, far, cf, loss[...], scale_ref[0], bias_ref[0]))


def last_body(scale_ref, bias_ref, img, mine, other, far, cn, cf, row):
    scale, bias = scale_ref[0], bias_ref[0]
    total = near_tile(img, mine, other, cn, jnp.zeros((256, 128), F32), scale, bias)
    row[...] = loss_row(tile(img, far, cf, total, scale, bias))


def near_part_body(c0, c1, c3, i0, i1, i3, part):
    part[...] = texts((c0, c1, c3), (i0, i1, i3), 0, 640)


def texts_body(c0, c1, c2, c3, n2, i0, i1, i2, i3, part, keep_a, send_a, keep_b, send_b, pair):
    g = texts((c0, c1, c2, c3), (i0, i1, i2, i3), 0, 384)
    keep_a[...] = g[:192, :]
    send_a[...] = g[192:, :].astype(BF16)
    g = part[...] + texts((n2,), (i2,), 0, 640)
    keep_b[...] = g[:256, :]
    send_b[...] = g[256:512, :].astype(BF16)
    pair[...] = g[512:, :]


def last_image_body(cn, cf, mine, other, far, row, out):
    send_image(out, image(cn, cf, mine, other, far), row[...])


def own_image_body(cn, cf, mine, other, far, out):
    out[...] = image(cn, cf, mine, other, far)


def merge_img_body(g_ref, l_ref, r1, r2, r3, own_ref, own_loss, m1, m2, m3):
    loss = l_ref[...] + (
        loss_sum(r1[256:, :256]) + loss_sum(r2[256:, :256]) + loss_sum(r3[256:, :256])
    )
    own_loss[...] = loss
    marks = loss_rows(loss)
    for j, out in enumerate((own_ref, m1, m2, m3)):
        lo, hi = U * j, U * (j + 1)
        total = g_ref[lo:hi, :] + (up(r1, lo, hi) + up(r2, lo, hi) + up(r3, lo, hi))
        out[:U, :] = total.astype(out.dtype)
        if j:
            out[U:, :] = jnp.zeros((8, total.shape[1]), BF16)
            out[U:, :256] = marks


def pack_body(*refs):
    out, at = refs[-1], 0
    for ref in refs[:-1]:
        n = min(ref.shape[0], out.shape[0] - at)
        out[at : at + n, :] = ref[:n, :]
        at += n
    if at < out.shape[0]:
        out[at:, :] = jnp.zeros((out.shape[0] - at, out.shape[1]), out.dtype)


def split_body(b1, b2, far, near):
    far[:U, :] = b2[:U, :]
    far[U:, :] = b1[...]
    near[:128, :] = b2[...]
    near[128:, :] = b1[...]


def step1_body(keep, got, out):
    out[...] = (keep[...] + got[...].astype(F32)).astype(BF16)


def step2_body(keep, got, w, two, one):
    two[:64, :] = (keep[:64, :] + (up(got, 0, 64) + up(w, 0, 64))).astype(BF16)
    two[64:, :] = (keep[64:128, :] + up(got, 64, 128)).astype(BF16)
    one[...] = (keep[128:, :] + (up(got, 128, 256) + up(w, 64, 192))).astype(BF16)


def step3_body(pair, v1, v2, out):
    out[...] = (pair[64:, :] + (up(v1, 64, 128) + up(v2, 64, 128))).astype(BF16)


def back_norm(g, raw, inv):
    unit = raw[...].astype(F32) * inv[...]
    return inv[...] * (g - unit * jnp.sum(unit * g, axis=-1, keepdims=True))


def finish_body(g_ref, l_ref, r1, r2, r3, raw_i, inv_i, pair, v1, v2, got, raw_t, inv_t, img_ref, txt_ref, loss_ref):
    g = g_ref[...] + (up(r1, 0, U) + up(r2, 0, U) + up(r3, 0, U))
    img_ref[...] = back_norm(g, raw_i, inv_i)
    loss = l_ref[:1, :U]
    for j, r in enumerate((r1, r2, r3)):
        loss = loss + loss_sum(r[U:, U * (j + 1) : U * (j + 2)])
    loss_ref[...] = loss
    g = pair[:64, :] + (up(v1, 0, 64) + up(v2, 0, 64) + got[...].astype(F32))
    txt_ref[...] = back_norm(g, raw_t, inv_t)


def on_device(picture, caption, scale, bias):
    rows, d = picture.shape
    img, txt, img_inv, txt_inv = call(
        "normalize", normalize_body,
        [shape(rows, d), shape(rows, d), shape(rows, 1, dtype=F32), shape(rows, 1, dtype=F32)],
        [pltpu.with_memory_space_constraint(a, pltpu.HBM) for a in (picture, caption)], specs=[HBM] * 2,
        scratch=[pltpu.VMEM((2, rows, d), BF16), pltpu.SemaphoreType.DMA((2,))],
    )

    def pack(name, n, parts, after=()):
        return call(name, pack_body, [shape(n, d)], parts, (), after)[0]

    pair = pack("pair", 128, (txt, swap(txt)))
    b2, b1 = ring(pair, 2), ring(pair, 1)
    f2, f1, f3 = first(img, 2), first(img, 1), first(img, 3)
    group = pack("group", 264, (img, f1, f2, f3))
    g1, g3, g2 = second(group, 1), second(group, 3), second(group, 2)
    groups = (group, g1, g2, g3)
    far_pack, near_mine = call(
        "pack", split_body, [shape(192, d), shape(256, d)], (b1, b2), (), (group,)
    )
    far_got = ring(far_pack, 2)
    near_other = swap(near_mine)

    sc = (scale, bias)
    far_mine = pack("far_mine", 192, (far_got,))
    far_other = swap(far_mine)
    other = pack("other_texts", 384, (near_other, pair), (far_mine,))
    near_c, near_l, last = [None] * 4, [None] * 4, ()
    for k in (0, 1, 3):
        near_c[k], near_l[k] = call(
            f"near{k}", functools.partial(near_body, k == 0), [shape(256, 640), shape(256, 128, dtype=F32)],
            (groups[k], near_mine, other), sc, last,
        )
        last = (near_l[k],)
    part = call(
        "near_part", near_part_body, [shape(640, d, dtype=F32)],
        (near_c[0], near_c[1], near_c[3], groups[0], groups[1], groups[3]), (), last,
    )[0]
    far = pack("far_texts", 384, (far_mine, far_other), (part,))
    far_c, sent, last = [None] * 4, [None] * 4, ()
    for k in (1, 3):
        far_c[k], sent[k] = call(
            f"far_image{k}", far_image_body, [shape(256, 384), shape(264, d)],
            (groups[k], near_mine, other, far, near_c[k], near_l[k]), sc, last,
        )
        last = (sent[k],)
    r1, r3 = second(sent[1], -1), second(sent[3], -3)
    far_c[0], row0 = call(
        "far_own", far_own_body, [shape(256, 384), shape(8, 256, dtype=F32)],
        (groups[0], far, near_l[0]), sc, last,
    )
    near_c[2], far_c[2], row2 = call(
        "last", last_body, [shape(256, 640), shape(256, 384), shape(8, 256, dtype=F32)],
        (groups[2], near_mine, other, far), sc, (row0,),
    )
    keep_a, send_a, keep_b, send_b, own_pair = call(
        "texts_grad", texts_body,
        [shape(192, d, dtype=F32), shape(192, d), shape(256, d, dtype=F32), shape(256, d), shape(128, d, dtype=F32)],
        (*far_c, near_c[2], *groups, part),
    )
    got_a = swap(send_a)
    sent[2] = call(
        "last_image", last_image_body, [shape(264, d)],
        (near_c[2], far_c[2], near_mine, other, far, row2), (), (send_a,),
    )[0]
    r2 = second(sent[2], -2)

    z1 = call("step1", step1_body, [shape(192, d)], (keep_a, got_a), (), (sent[2],))[0]
    w = ring(z1, -2)
    got_b = swap(send_b)
    p0 = call(
        "own_image", own_image_body, [shape(256, d, dtype=F32)],
        (near_c[0], far_c[0], near_mine, other, far), (), (z1,),
    )[0]
    two, one = call("step2", step2_body, [shape(128, d)] * 2, (keep_b, got_b, w), (), (p0,))
    v2, v1 = ring(two, -2), ring(one, -1)
    own_img, own_loss, m1, m2, m3 = call(
        "merge_img", merge_img_body,
        [shape(rows, d, dtype=F32), shape(8, 256, dtype=F32)] + [shape(rows + 8, d)] * 3,
        (p0, row0, r1, r2, r3), (), (one,),
    )
    q1, q3, q2 = first(m1, -1), first(m3, -3), first(m2, -2)
    z3 = call("step3", step3_body, [shape(64, d)], (own_pair, v1, v2), (), (m3,))[0]
    got_c = swap(z3)
    grad_img, grad_txt, loss_out = call(
        "finish", finish_body,
        [shape(rows, d, dtype=F32), shape(rows, d, dtype=F32), shape(1, rows, dtype=F32)],
        (own_img, own_loss, q1, q2, q3, picture, img_inv, own_pair, v1, v2, got_c, caption, txt_inv),
    )
    return grad_img, grad_txt, loss_out.reshape(rows)


def solution(mesh):
    torus = Mesh(mesh.devices.reshape(NX, NC, NZ, NY), AXES)
    return jax.shard_map(
        on_device,
        mesh=torus,
        in_specs=(P(AXES, None), P(AXES, None), P(), P()),
        out_specs=(P(AXES, None), P(AXES, None), P(AXES)),
        check_vma=False,
    )
```

```python
import functools

import jax
import jax.numpy as jnp
from jax import lax
from jax.experimental import pallas as pl
from jax.experimental.pallas import tpu as pltpu
from jax.sharding import Mesh
from jax.sharding import PartitionSpec as P

AXES = ("x", "core", "z", "y")
NX, NC, NZ, NY = 4, 2, 8, 4
U = 64
EPS = 1e-06
F32 = jnp.float32
BF16 = jnp.bfloat16
MIB = 1 << 20
VMEM = pl.BlockSpec(memory_space=pltpu.VMEM)
SMEM = pl.BlockSpec(memory_space=pltpu.SMEM)
ANY = pl.BlockSpec(memory_space=pl.ANY)
HBM = pl.BlockSpec(memory_space=pltpu.HBM)


def device(x, core, z, y):
    return ((x % NX * NC + core) * NZ + z % NZ) * NY + y % NY


def permutation(move):
    return [
        (device(x, c, z, y), device(*move(x, c, z, y)))
        for x in range(NX)
        for c in range(NC)
        for z in range(NZ)
        for y in range(NY)
    ]


def first(a, s):
    return lax.ppermute(
        a, AXES, permutation(lambda x, c, z, y: (x, c, z, y + s) if c else (x + s, c, z, y))
    )


def second(a, s):
    return lax.ppermute(
        a, AXES, permutation(lambda x, c, z, y: (x + s, c, z, y) if c else (x, c, z, y + s))
    )


def ring(a, s):
    return lax.ppermute(a, AXES, permutation(lambda x, c, z, y: (x, c, z - s if c else z + s, y)))


def swap(a):
    return lax.ppermute(a, AXES, permutation(lambda x, c, z, y: (x, 1 - c, z, y)))


def call(name, body, outs, ins, scalars=(), after=(), specs=None, scratch=()):
    n_out, n_in = len(outs), len(ins) + len(scalars)

    def kernel(*refs):
        used = refs[:n_in] + refs[n_in + len(after) :]
        body(*used)

    return pl.pallas_call(
        kernel,
        out_shape=outs,
        in_specs=[SMEM] * len(scalars) + (specs or [VMEM] * len(ins)) + [ANY] * len(after),
        out_specs=[VMEM] * n_out,
        scratch_shapes=list(scratch),
        name=name,
        cost_estimate=pl.CostEstimate(flops=1, bytes_accessed=1, transcendentals=0),
        compiler_params=pltpu.CompilerParams(vmem_limit_bytes=20 * MIB),
    )(*scalars, *ins, *after)


def shape(*dims, dtype=BF16):
    return jax.ShapeDtypeStruct(dims, dtype)


def up(ref, lo, hi):
    return ref[lo:hi, :].astype(F32)


def normalize_body(img_ref, txt_ref, img_unit, txt_unit, img_inv, txt_inv, raw_ref, sem):
    copies = [
        pltpu.make_async_copy(src, raw_ref.at[i], sem.at[i])
        for i, src in enumerate((img_ref, txt_ref))
    ]
    for copy in copies:
        copy.start()
    for i, (unit, inv) in enumerate(((img_unit, img_inv), (txt_unit, txt_inv))):
        copies[i].wait()
        v = raw_ref[i].astype(F32)
        r = lax.rsqrt(jnp.sum(v * v, axis=-1, keepdims=True) + EPS)
        unit[...] = (v * r).astype(BF16)
        inv[...] = r


def split3(v):
    hi = v.astype(BF16).astype(F32)
    mid = (v - hi).astype(BF16).astype(F32)
    return hi, mid, v - hi - mid


def loss_rows(total):
    hi, mid, low = split3(total)
    at = lax.broadcasted_iota(jnp.int32, total.shape, 0)
    return jnp.where(at == 0, hi, jnp.where(at == 1, mid, jnp.where(at == 2, low, 0.0))).astype(BF16)


def loss_sum(rows):
    return jnp.sum(rows.astype(F32), axis=0, keepdims=True)


def entry(img, txt, scale, bias, match=None):
    dots = lax.dot_general(img, txt, (((1,), (1,)), ((), ())), preferred_element_type=F32)
    logits = dots * scale + bias
    if match is not None:
        logits = jnp.where(match, -logits, logits)
    e = jnp.exp(logits)
    u = 1.0 + e
    inv = 1.0 / u
    softplus = jnp.log(u) + (e - (u - 1.0)) * inv
    weight = scale * (e * inv)
    if match is not None:
        weight = jnp.where(match, -weight, weight)
    return weight.astype(BF16), softplus


def fold(v):
    total = v[:, :128]
    for n in range(1, v.shape[1] // 128):
        total = total + v[:, 128 * n : 128 * (n + 1)]
    return total


def texts(coeffs, imgs, lo, hi):
    total = None
    for c, s in zip(coeffs, imgs):
        part = lax.dot_general(
            c[:, lo:hi], s[:256, :], (((0,), (0,)), ((), ())), preferred_element_type=F32
        )
        total = part if total is None else total + part
    return total


def tile(img, txt_ref, coeff_ref, total, scale, bias, own=False):
    for lo, hi in ((0, 256), (256, 384)):
        match = None
        if own and lo == 256:
            r = lax.broadcasted_iota(jnp.int32, (256, 128), 0)
            c = lax.broadcasted_iota(jnp.int32, (256, 128), 1)
            match = (r == c) & (r < U)
        weight, softplus = entry(img[:256, :], txt_ref[lo:hi, :], scale, bias, match)
        coeff_ref[:, lo:hi] = weight
        total = total + fold(softplus)
    return total


def near_tile(img, mine_ref, other_ref, coeff_ref, total, scale, bias, own=False):
    weight, softplus = entry(img[:256, :], mine_ref[...], scale, bias)
    coeff_ref[:, :256] = weight
    total = total + fold(softplus)
    return tile(img, other_ref, coeff_ref.at[:, 256:], total, scale, bias, own)


def loss_row(total):
    column = jnp.broadcast_to(jnp.sum(total, axis=1, keepdims=True), (256, 128))
    return jnp.transpose(column)[:8, :]


def near_image(cn, mine, other):
    g = jnp.dot(cn[:, :256], mine[...], preferred_element_type=F32)
    return g + jnp.dot(cn[:, 256:], other[...], preferred_element_type=F32)


def far_image(cf, far):
    return jnp.dot(cf[...], far[...], preferred_element_type=F32)


def own_near_body(scale_ref, bias_ref, img, mine, other, cn, loss, part, g):
    zero = jnp.zeros((256, 128), F32)
    loss[...] = near_tile(img, mine, other, cn, zero, scale_ref[0], bias_ref[0], True)
    part[...] = texts((cn,), (img,), 0, 640)
    g[...] = near_image(cn, mine, other)


def near_pair_body(scale_ref, bias_ref, i1, i3, mine, other, part0, n1, n3, l1, l3, part):
    zero = jnp.zeros((256, 128), F32)
    for i, n, l in ((i1, n1, l1), (i3, n3, l3)):
        l[...] = near_tile(i, mine, other, n, zero, scale_ref[0], bias_ref[0])
    part[...] = part0[...] + texts((n1, n3), (i1, i3), 0, 640)


def far_body(scale_ref, bias_ref, i0, i1, i3, far, l0, l1, l3, c0, c1, c3, rows):
    for n, (i, l, c) in enumerate(((i0, l0, c0), (i1, l1, c1), (i3, l3, c3))):
        total = tile(i, far, c, l[...], scale_ref[0], bias_ref[0])
        rows[:, 256 * n : 256 * (n + 1)] = loss_row(total)


def last_body(scale_ref, bias_ref, i0, i1, i2, i3, mine, other, far, c0, c1, c3, part, n2, c2, row, keep_a, send_a, keep_b, send_b, pair):
    scale, bias = scale_ref[0], bias_ref[0]
    total = near_tile(i2, mine, other, n2, jnp.zeros((256, 128), F32), scale, bias)
    row[...] = loss_row(tile(i2, far, c2, total, scale, bias))
    g = texts((c0, c1, c2, c3), (i0, i1, i2, i3), 0, 384)
    keep_a[...] = g[:192, :]
    send_a[...] = g[192:, :].astype(BF16)
    g = part[...] + texts((n2,), (i2,), 0, 640)
    keep_b[...] = g[:256, :]
    send_b[...] = g[256:512, :].astype(BF16)
    pair[...] = g[512:, :]


def image_body(at, cn, cf, mine, other, far, row, out):
    g = near_image(cn, mine, other) + far_image(cf, far)
    out[:256, :] = g.astype(BF16)
    out[256:, :] = jnp.zeros((8, g.shape[1]), BF16)
    out[256:, :256] = loss_rows(row[:, 256 * at : 256 * (at + 1)])


def own_image_body(near, cf, far, out):
    out[...] = near[...] + far_image(cf, far)


def merge_img_body(g_ref, l_ref, r1, r2, r3, own_ref, own_loss, m1, m2, m3):
    loss = l_ref[:, :256] + (
        loss_sum(r1[256:, :256]) + loss_sum(r2[256:, :256]) + loss_sum(r3[256:, :256])
    )
    own_loss[...] = loss
    marks = loss_rows(loss)
    for j, out in enumerate((own_ref, m1, m2, m3)):
        lo, hi = U * j, U * (j + 1)
        total = g_ref[lo:hi, :] + (up(r1, lo, hi) + up(r2, lo, hi) + up(r3, lo, hi))
        out[:U, :] = total.astype(out.dtype)
        if j:
            out[U:, :] = jnp.zeros((8, total.shape[1]), BF16)
            out[U:, :256] = marks


def pack_body(*refs):
    out, at = refs[-1], 0
    for ref in refs[:-1]:
        n = min(ref.shape[0], out.shape[0] - at)
        out[at : at + n, :] = ref[:n, :]
        at += n
    if at < out.shape[0]:
        out[at:, :] = jnp.zeros((out.shape[0] - at, out.shape[1]), out.dtype)


def split_body(b1, b2, far, near):
    far[:U, :] = b2[:U, :]
    far[U:, :] = b1[...]
    near[:128, :] = b2[...]
    near[128:, :] = b1[...]


def step1_body(keep, got, out):
    out[...] = (keep[...] + got[...].astype(F32)).astype(BF16)


def step2_body(keep, got, w, two, one):
    two[:64, :] = (keep[:64, :] + (up(got, 0, 64) + up(w, 0, 64))).astype(BF16)
    two[64:, :] = (keep[64:128, :] + up(got, 64, 128)).astype(BF16)
    one[...] = (keep[128:, :] + (up(got, 128, 256) + up(w, 64, 192))).astype(BF16)


def step3_body(pair, v1, v2, out):
    out[...] = (pair[64:, :] + (up(v1, 64, 128) + up(v2, 64, 128))).astype(BF16)


def back_norm(g, raw, inv):
    unit = raw[...].astype(F32) * inv[...]
    return inv[...] * (g - unit * jnp.sum(unit * g, axis=-1, keepdims=True))


def finish_body(g_ref, l_ref, r1, r2, r3, raw_i, inv_i, pair, v1, v2, got, raw_t, inv_t, img_ref, txt_ref, loss_ref):
    g = g_ref[...] + (up(r1, 0, U) + up(r2, 0, U) + up(r3, 0, U))
    img_ref[...] = back_norm(g, raw_i, inv_i)
    loss = l_ref[:1, :U]
    for j, r in enumerate((r1, r2, r3)):
        loss = loss + loss_sum(r[U:, U * (j + 1) : U * (j + 2)])
    loss_ref[...] = loss
    g = pair[:64, :] + (up(v1, 0, 64) + up(v2, 0, 64) + got[...].astype(F32))
    txt_ref[...] = back_norm(g, raw_t, inv_t)


def on_device(picture, caption, scale, bias):
    rows, d = picture.shape
    img, txt, img_inv, txt_inv = call(
        "normalize", normalize_body,
        [shape(rows, d), shape(rows, d), shape(rows, 1, dtype=F32), shape(rows, 1, dtype=F32)],
        [pltpu.with_memory_space_constraint(a, pltpu.HBM) for a in (picture, caption)], specs=[HBM] * 2,
        scratch=[pltpu.VMEM((2, rows, d), BF16), pltpu.SemaphoreType.DMA((2,))],
    )

    def pack(name, n, parts, after=()):
        return call(name, pack_body, [shape(n, d)], parts, (), after)[0]

    pair = pack("pair", 128, (txt, swap(txt)))
    b2, b1 = ring(pair, 2), ring(pair, 1)
    f2, f1, f3 = first(img, 2), first(img, 1), first(img, 3)
    group = pack("group", 264, (img, f1, f2, f3))
    g1, g3, g2 = second(group, 1), second(group, 3), second(group, 2)
    groups = (group, g1, g2, g3)
    far_pack, near_mine = call(
        "pack", split_body, [shape(192, d), shape(256, d)], (b1, b2), (), (group,)
    )
    far_got = ring(far_pack, 2)
    near_other = swap(near_mine)

    sc = (scale, bias)
    other = pack("other_texts", 384, (near_other, pair))
    own_c, own_l, part0, own_near = call(
        "own_near", own_near_body,
        [shape(256, 640), shape(256, 128, dtype=F32), shape(640, d, dtype=F32), shape(256, d, dtype=F32)],
        (group, near_mine, other), sc,
    )
    far_mine = pack("far_mine", 192, (far_got,), (own_l,))
    n1, n3, l1, l3, part = call(
        "near_pair", near_pair_body,
        [shape(256, 640)] * 2 + [shape(256, 128, dtype=F32)] * 2 + [shape(640, d, dtype=F32)],
        (g1, g3, near_mine, other, part0), sc, (far_mine,),
    )
    far = pack("far_texts", 384, (far_mine, swap(far_mine)), (l1,))
    c0, c1, c3, rows013 = call(
        "far", far_body, [shape(256, 384)] * 3 + [shape(8, 768, dtype=F32)],
        (group, g1, g3, far, own_l, l1, l3), sc,
    )
    n2, c2, row2, keep_a, send_a, keep_b, send_b, own_pair = call(
        "last", last_body,
        [shape(256, 640), shape(256, 384), shape(8, 256, dtype=F32)]
        + [shape(192, d, dtype=F32), shape(192, d), shape(256, d, dtype=F32), shape(256, d), shape(128, d, dtype=F32)],
        (*groups, near_mine, other, far, c0, c1, c3, part), sc,
    )
    got_a, got_b = swap(send_a), swap(send_b)

    def sent(name, at, cn, cf, row, after):
        return call(
            name, functools.partial(image_body, at), [shape(264, d)],
            (cn, cf, near_mine, other, far, row), (), after,
        )[0]

    p1 = sent("image1", 1, n1, c1, rows013, (send_a,))
    z1 = call("step1", step1_body, [shape(192, d)], (keep_a, got_a), (), (p1, got_b))[0]
    w = ring(z1, -2)
    p3 = sent("image3", 2, n3, c3, rows013, (z1,))
    p2 = sent("image2", 0, n2, c2, row2, (p3,))
    r1, r3, r2 = second(p1, -1), second(p3, -3), second(p2, -2)
    p0 = call(
        "own_image", own_image_body, [shape(256, d, dtype=F32)], (own_near, c0, far), (), (p2,)
    )[0]
    two, one = call("step2", step2_body, [shape(128, d)] * 2, (keep_b, got_b, w), (), (p0,))
    v2, v1 = ring(two, -2), ring(one, -1)
    own_img, own_loss, m1, m2, m3 = call(
        "merge_img", merge_img_body,
        [shape(rows, d, dtype=F32), shape(8, 256, dtype=F32)] + [shape(rows + 8, d)] * 3,
        (p0, rows013, r1, r2, r3), (), (one,),
    )
    q1, q3, q2 = first(m1, -1), first(m3, -3), first(m2, -2)
    z3 = call("step3", step3_body, [shape(64, d)], (own_pair, v1, v2), (), (m3,))[0]
    got_c = swap(z3)
    grad_img, grad_txt, loss_out = call(
        "finish", finish_body,
        [shape(rows, d, dtype=F32), shape(rows, d, dtype=F32), shape(1, rows, dtype=F32)],
        (own_img, own_loss, q1, q2, q3, picture, img_inv, own_pair, v1, v2, got_c, caption, txt_inv),
    )
    return grad_img, grad_txt, loss_out.reshape(rows)


def solution(mesh):
    torus = Mesh(mesh.devices.reshape(NX, NC, NZ, NY), AXES)
    return jax.shard_map(
        on_device,
        mesh=torus,
        in_specs=(P(AXES, None), P(AXES, None), P(), P()),
        out_specs=(P(AXES, None), P(AXES, None), P(AXES)),
        check_vma=False,
    )
```

```python
import functools

import jax
import jax.numpy as jnp
from jax import lax
from jax.experimental import pallas as pl
from jax.experimental.pallas import tpu as pltpu
from jax.sharding import Mesh
from jax.sharding import PartitionSpec as P

AXES = ("x", "core", "z", "y")
NX, NC, NZ, NY = 4, 2, 8, 4
U = 64
EPS = 1e-06
F32 = jnp.float32
BF16 = jnp.bfloat16
MIB = 1 << 20
VMEM = pl.BlockSpec(memory_space=pltpu.VMEM)
SMEM = pl.BlockSpec(memory_space=pltpu.SMEM)
ANY = pl.BlockSpec(memory_space=pl.ANY)
HBM = pl.BlockSpec(memory_space=pltpu.HBM)


def device(x, core, z, y):
    return ((x % NX * NC + core) * NZ + z % NZ) * NY + y % NY


def permutation(move):
    return [
        (device(x, c, z, y), device(*move(x, c, z, y)))
        for x in range(NX)
        for c in range(NC)
        for z in range(NZ)
        for y in range(NY)
    ]


def first(a, s):
    return lax.ppermute(
        a, AXES, permutation(lambda x, c, z, y: (x, c, z, y + s) if c else (x + s, c, z, y))
    )


def second(a, s):
    return lax.ppermute(
        a, AXES, permutation(lambda x, c, z, y: (x + s, c, z, y) if c else (x, c, z, y + s))
    )


def ring(a, s):
    return lax.ppermute(a, AXES, permutation(lambda x, c, z, y: (x, c, z - s if c else z + s, y)))


def swap(a):
    return lax.ppermute(a, AXES, permutation(lambda x, c, z, y: (x, 1 - c, z, y)))


def call(name, body, outs, ins, scalars=(), after=(), specs=None, scratch=()):
    n_out, n_in = len(outs), len(ins) + len(scalars)

    def kernel(*refs):
        used = refs[:n_in] + refs[n_in + len(after) :]
        body(*used)

    return pl.pallas_call(
        kernel,
        out_shape=outs,
        in_specs=[SMEM] * len(scalars) + (specs or [VMEM] * len(ins)) + [ANY] * len(after),
        out_specs=[VMEM] * n_out,
        scratch_shapes=list(scratch),
        name=name,
        cost_estimate=pl.CostEstimate(flops=1, bytes_accessed=1, transcendentals=0),
        compiler_params=pltpu.CompilerParams(vmem_limit_bytes=20 * MIB),
    )(*scalars, *ins, *after)


def shape(*dims, dtype=BF16):
    return jax.ShapeDtypeStruct(dims, dtype)


def up(ref, lo, hi):
    return ref[lo:hi, :].astype(F32)


def normalize_body(img_ref, txt_ref, img_unit, txt_unit, img_inv, txt_inv, raw_ref, sem):
    copies = [
        pltpu.make_async_copy(src, raw_ref.at[i], sem.at[i])
        for i, src in enumerate((img_ref, txt_ref))
    ]
    for copy in copies:
        copy.start()
    for i, (unit, inv) in enumerate(((img_unit, img_inv), (txt_unit, txt_inv))):
        copies[i].wait()
        v = raw_ref[i].astype(F32)
        r = lax.rsqrt(jnp.sum(v * v, axis=-1, keepdims=True) + EPS)
        unit[...] = (v * r).astype(BF16)
        inv[...] = r


def split3(v):
    hi = v.astype(BF16).astype(F32)
    mid = (v - hi).astype(BF16).astype(F32)
    return hi, mid, v - hi - mid


def loss_rows(total):
    hi, mid, low = split3(total)
    at = lax.broadcasted_iota(jnp.int32, total.shape, 0)
    return jnp.where(at == 0, hi, jnp.where(at == 1, mid, jnp.where(at == 2, low, 0.0))).astype(BF16)


def loss_sum(rows):
    return jnp.sum(rows.astype(F32), axis=0, keepdims=True)


def entry(img, txt, scale, bias, match=None):
    dots = lax.dot_general(img, txt, (((1,), (1,)), ((), ())), preferred_element_type=F32)
    logits = dots * scale + bias
    if match is not None:
        logits = jnp.where(match, -logits, logits)
    e = jnp.exp(logits)
    u = 1.0 + e
    inv = 1.0 / u
    softplus = jnp.log(u) + (e - (u - 1.0)) * inv
    weight = scale * (e * inv)
    if match is not None:
        weight = jnp.where(match, -weight, weight)
    return weight.astype(BF16), softplus


def fold(v):
    total = v[:, :128]
    for n in range(1, v.shape[1] // 128):
        total = total + v[:, 128 * n : 128 * (n + 1)]
    return total


def texts(coeffs, imgs, lo, hi):
    total = None
    for c, s in zip(coeffs, imgs):
        part = lax.dot_general(
            c[:, lo:hi], s[:256, :], (((0,), (0,)), ((), ())), preferred_element_type=F32
        )
        total = part if total is None else total + part
    return total


def tile(img, txt_ref, coeff_ref, total, scale, bias, own=False):
    for lo, hi in ((0, 256), (256, 384)):
        match = None
        if own and lo == 256:
            r = lax.broadcasted_iota(jnp.int32, (256, 128), 0)
            c = lax.broadcasted_iota(jnp.int32, (256, 128), 1)
            match = (r == c) & (r < U)
        weight, softplus = entry(img[:256, :], txt_ref[lo:hi, :], scale, bias, match)
        coeff_ref[:, lo:hi] = weight
        total = total + fold(softplus)
    return total


def near_tile(img, mine_ref, other_ref, coeff_ref, total, scale, bias, own=False):
    weight, softplus = entry(img[:256, :], mine_ref[...], scale, bias)
    coeff_ref[:, :256] = weight
    total = total + fold(softplus)
    return tile(img, other_ref, coeff_ref.at[:, 256:], total, scale, bias, own)


def loss_row(total):
    column = jnp.broadcast_to(jnp.sum(total, axis=1, keepdims=True), (256, 128))
    return jnp.transpose(column)[:8, :]


def near_image(cn, mine, other):
    g = jnp.dot(cn[:, :256], mine[...], preferred_element_type=F32)
    return g + jnp.dot(cn[:, 256:], other[...], preferred_element_type=F32)


def far_image(cf, far):
    return jnp.dot(cf[...], far[...], preferred_element_type=F32)


def mine_body(scale_ref, bias_ref, img_ref, txt_ref, coeff_ref, loss_ref):
    weight, softplus = entry(img_ref[:256, :], txt_ref[...], scale_ref[0], bias_ref[0])
    coeff_ref[...] = weight
    loss_ref[...] = fold(softplus)


def other_body(scale_ref, bias_ref, i0, i1, i3, m0, m1, m3, l0, l1, l3, txt_ref, n0, n1, n3, t0, t1, t3, part):
    groups = ((i0, m0, l0, n0, t0), (i1, m1, l1, n1, t1), (i3, m3, l3, n3, t3))
    for k, (i, m, l, n, t) in enumerate(groups):
        n[:, :256] = m[...]
        t[...] = tile(i, txt_ref, n.at[:, 256:], l[...], scale_ref[0], bias_ref[0], k == 0)
    part[...] = texts((n0, n1, n3), (i0, i1, i3), 0, 640)


def near_images_body(n0, n1, n3, mine, other, g0, g1, g3):
    for n, g in ((n0, g0), (n1, g1), (n3, g3)):
        g[...] = near_image(n, mine, other)


def far_body(scale_ref, bias_ref, i0, i1, i3, far, l0, l1, l3, c0, c1, c3, rows):
    for n, (i, l, c) in enumerate(((i0, l0, c0), (i1, l1, c1), (i3, l3, c3))):
        total = tile(i, far, c, l[...], scale_ref[0], bias_ref[0])
        rows[:, 256 * n : 256 * (n + 1)] = loss_row(total)


def last_body(scale_ref, bias_ref, i0, i1, i2, i3, mine, other, far, c0, c1, c3, part, n2, c2, row, keep_a, send_a, keep_b, send_b, pair):
    scale, bias = scale_ref[0], bias_ref[0]
    total = near_tile(i2, mine, other, n2, jnp.zeros((256, 128), F32), scale, bias)
    row[...] = loss_row(tile(i2, far, c2, total, scale, bias))
    g = texts((c0, c1, c2, c3), (i0, i1, i2, i3), 0, 384)
    keep_a[...] = g[:192, :]
    send_a[...] = g[192:, :].astype(BF16)
    g = part[...] + texts((n2,), (i2,), 0, 640)
    keep_b[...] = g[:256, :]
    send_b[...] = g[256:512, :].astype(BF16)
    pair[...] = g[512:, :]


def send_image(out, g, row):
    out[:256, :] = g.astype(BF16)
    out[256:, :] = jnp.zeros((8, g.shape[1]), BF16)
    out[256:, :256] = loss_rows(row)


def image_body(at, near, cf, far, row, out):
    send_image(out, near[...] + far_image(cf, far), row[:, 256 * at : 256 * (at + 1)])


def last_image_body(cn, cf, mine, other, far, row, out):
    send_image(out, near_image(cn, mine, other) + far_image(cf, far), row[...])


def own_image_body(near, cf, far, out):
    out[...] = near[...] + far_image(cf, far)


def merge_img_body(g_ref, l_ref, r1, r2, r3, own_ref, own_loss, m1, m2, m3):
    loss = l_ref[:, :256] + (
        loss_sum(r1[256:, :256]) + loss_sum(r2[256:, :256]) + loss_sum(r3[256:, :256])
    )
    own_loss[...] = loss
    marks = loss_rows(loss)
    for j, out in enumerate((own_ref, m1, m2, m3)):
        lo, hi = U * j, U * (j + 1)
        total = g_ref[lo:hi, :] + (up(r1, lo, hi) + up(r2, lo, hi) + up(r3, lo, hi))
        out[:U, :] = total.astype(out.dtype)
        if j:
            out[U:, :] = jnp.zeros((8, total.shape[1]), BF16)
            out[U:, :256] = marks


def pack_body(*refs):
    out, at = refs[-1], 0
    for ref in refs[:-1]:
        n = min(ref.shape[0], out.shape[0] - at)
        out[at : at + n, :] = ref[:n, :]
        at += n
    if at < out.shape[0]:
        out[at:, :] = jnp.zeros((out.shape[0] - at, out.shape[1]), out.dtype)


def split_body(b1, b2, half, near):
    half[...] = b2[:U, :]
    near[:128, :] = b2[...]
    near[128:, :] = b1[...]


def step1_body(keep, got, out):
    out[...] = (keep[...] + got[...].astype(F32)).astype(BF16)


def step2_body(keep, got, w, two, one):
    two[:64, :] = (keep[:64, :] + (up(got, 0, 64) + up(w, 0, 64))).astype(BF16)
    two[64:, :] = (keep[64:128, :] + up(got, 64, 128)).astype(BF16)
    one[...] = (keep[128:, :] + (up(got, 128, 256) + up(w, 64, 192))).astype(BF16)


def step3_body(pair, v1, v2, out):
    out[...] = (pair[64:, :] + (up(v1, 64, 128) + up(v2, 64, 128))).astype(BF16)


def back_norm(g, raw, inv):
    unit = raw[...].astype(F32) * inv[...]
    return inv[...] * (g - unit * jnp.sum(unit * g, axis=-1, keepdims=True))


def finish_body(g_ref, l_ref, r1, r2, r3, raw_i, inv_i, pair, v1, v2, got, raw_t, inv_t, img_ref, txt_ref, loss_ref):
    g = g_ref[...] + (up(r1, 0, U) + up(r2, 0, U) + up(r3, 0, U))
    img_ref[...] = back_norm(g, raw_i, inv_i)
    loss = l_ref[:1, :U]
    for j, r in enumerate((r1, r2, r3)):
        loss = loss + loss_sum(r[U:, U * (j + 1) : U * (j + 2)])
    loss_ref[...] = loss
    g = pair[:64, :] + (up(v1, 0, 64) + up(v2, 0, 64) + got[...].astype(F32))
    txt_ref[...] = back_norm(g, raw_t, inv_t)


def on_device(picture, caption, scale, bias):
    rows, d = picture.shape
    img, txt, img_inv, txt_inv = call(
        "normalize", normalize_body,
        [shape(rows, d), shape(rows, d), shape(rows, 1, dtype=F32), shape(rows, 1, dtype=F32)],
        [pltpu.with_memory_space_constraint(a, pltpu.HBM) for a in (picture, caption)], specs=[HBM] * 2,
        scratch=[pltpu.VMEM((2, rows, d), BF16), pltpu.SemaphoreType.DMA((2,))],
    )

    def pack(name, n, parts, after=()):
        return call(name, pack_body, [shape(n, d)], parts, (), after)[0]

    pair = pack("pair", 128, (txt, swap(txt)))
    b2, b1 = ring(pair, 2), ring(pair, 1)
    f2, f1, f3 = first(img, 2), first(img, 1), first(img, 3)
    group = pack("group", 264, (img, f1, f2, f3))
    g1, g3, g2 = second(group, 1), second(group, 3), second(group, 2)
    groups = (group, g1, g2, g3)
    half, near_mine = call(
        "pack", split_body, [shape(64, d), shape(256, d)], (b1, b2), (), (group,)
    )
    near_other = swap(near_mine)
    b3, b4 = ring(b2, 1), ring(half, 2)

    sc = (scale, bias)
    mine_c, mine_l, last = {}, {}, ()
    for k in (0, 1, 3):
        mine_c[k], mine_l[k] = call(
            f"mine{k}", mine_body, [shape(256, 256), shape(256, 128, dtype=F32)],
            (groups[k], near_mine), sc, last,
        )
        last = (mine_l[k],)
    other = pack("other_texts", 384, (near_other, pair), last)
    n0, n1, n3, l0, l1, l3, part = call(
        "other", other_body,
        [shape(256, 640)] * 3 + [shape(256, 128, dtype=F32)] * 3 + [shape(640, d, dtype=F32)],
        (group, g1, g3, *mine_c.values(), *mine_l.values(), other), sc,
    )
    far_mine = pack("far_mine", 192, (b4, b3), (l0,))
    far_other = swap(far_mine)
    t0, t1, t3 = call(
        "near_images", near_images_body, [shape(256, d, dtype=F32)] * 3,
        (n0, n1, n3, near_mine, other), (), (far_mine,),
    )
    far = pack("far_texts", 384, (far_mine, far_other), (t0,))
    c0, c1, c3, rows013 = call(
        "far", far_body, [shape(256, 384)] * 3 + [shape(8, 768, dtype=F32)],
        (group, g1, g3, far, l0, l1, l3), sc,
    )
    n2, c2, row2, keep_a, send_a, keep_b, send_b, own_pair = call(
        "last", last_body,
        [shape(256, 640), shape(256, 384), shape(8, 256, dtype=F32)]
        + [shape(192, d, dtype=F32), shape(192, d), shape(256, d, dtype=F32), shape(256, d), shape(128, d, dtype=F32)],
        (*groups, near_mine, other, far, c0, c1, c3, part), sc,
    )
    got_a, got_b = swap(send_a), swap(send_b)

    def sent(name, at, near, cf, after):
        return call(
            name, functools.partial(image_body, at), [shape(264, d)],
            (near, cf, far, rows013), (), after,
        )[0]

    p1 = sent("image1", 1, t1, c1, (send_a,))
    z1 = call("step1", step1_body, [shape(192, d)], (keep_a, got_a), (), (p1, got_b))[0]
    w = ring(z1, -2)
    p3 = sent("image3", 2, t3, c3, (z1,))
    p2 = call(
        "image2", last_image_body, [shape(264, d)], (n2, c2, near_mine, other, far, row2), (), (p3,)
    )[0]
    r1, r3, r2 = second(p1, -1), second(p3, -3), second(p2, -2)
    p0 = call(
        "own_image", own_image_body, [shape(256, d, dtype=F32)], (t0, c0, far), (), (p2,)
    )[0]
    two, one = call("step2", step2_body, [shape(128, d)] * 2, (keep_b, got_b, w), (), (p0,))
    v2, v1 = ring(two, -2), ring(one, -1)
    own_img, own_loss, m1, m2, m3 = call(
        "merge_img", merge_img_body,
        [shape(rows, d, dtype=F32), shape(8, 256, dtype=F32)] + [shape(rows + 8, d)] * 3,
        (p0, rows013, r1, r2, r3), (), (one,),
    )
    q1, q3, q2 = first(m1, -1), first(m3, -3), first(m2, -2)
    z3 = call("step3", step3_body, [shape(64, d)], (own_pair, v1, v2), (), (m3,))[0]
    got_c = swap(z3)
    grad_img, grad_txt, loss_out = call(
        "finish", finish_body,
        [shape(rows, d, dtype=F32), shape(rows, d, dtype=F32), shape(1, rows, dtype=F32)],
        (own_img, own_loss, q1, q2, q3, picture, img_inv, own_pair, v1, v2, got_c, caption, txt_inv),
    )
    return grad_img, grad_txt, loss_out.reshape(rows)


def solution(mesh):
    torus = Mesh(mesh.devices.reshape(NX, NC, NZ, NY), AXES)
    return jax.shard_map(
        on_device,
        mesh=torus,
        in_specs=(P(AXES, None), P(AXES, None), P(), P()),
        out_specs=(P(AXES, None), P(AXES, None), P(AXES)),
        check_vma=False,
    )
```

```python
import functools

import jax
import jax.numpy as jnp
from jax import lax
from jax.experimental import pallas as pl
from jax.experimental.pallas import tpu as pltpu
from jax.sharding import Mesh
from jax.sharding import PartitionSpec as P

AXES = ("x", "core", "z", "y")
NX, NC, NZ, NY = 4, 2, 8, 4
U = 64
EPS = 1e-06
F32 = jnp.float32
BF16 = jnp.bfloat16
MIB = 1 << 20
VMEM = pl.BlockSpec(memory_space=pltpu.VMEM)
SMEM = pl.BlockSpec(memory_space=pltpu.SMEM)
ANY = pl.BlockSpec(memory_space=pl.ANY)
HBM = pl.BlockSpec(memory_space=pltpu.HBM)


def device(x, core, z, y):
    return ((x % NX * NC + core) * NZ + z % NZ) * NY + y % NY


def permutation(move):
    return [
        (device(x, c, z, y), device(*move(x, c, z, y)))
        for x in range(NX)
        for c in range(NC)
        for z in range(NZ)
        for y in range(NY)
    ]


def first(a, s):
    return lax.ppermute(
        a, AXES, permutation(lambda x, c, z, y: (x, c, z, y + s) if c else (x + s, c, z, y))
    )


def second(a, s):
    return lax.ppermute(
        a, AXES, permutation(lambda x, c, z, y: (x + s, c, z, y) if c else (x, c, z, y + s))
    )


def ring(a, s):
    return lax.ppermute(a, AXES, permutation(lambda x, c, z, y: (x, c, z - s if c else z + s, y)))


def swap(a):
    return lax.ppermute(a, AXES, permutation(lambda x, c, z, y: (x, 1 - c, z, y)))


def call(name, body, outs, ins, scalars=(), after=(), specs=None, scratch=()):
    n_out, n_in = len(outs), len(ins) + len(scalars)

    def kernel(*refs):
        used = refs[:n_in] + refs[n_in + len(after) :]
        body(*used)

    return pl.pallas_call(
        kernel,
        out_shape=outs,
        in_specs=[SMEM] * len(scalars) + (specs or [VMEM] * len(ins)) + [ANY] * len(after),
        out_specs=[VMEM] * n_out,
        scratch_shapes=list(scratch),
        name=name,
        cost_estimate=pl.CostEstimate(flops=1, bytes_accessed=1, transcendentals=0),
        compiler_params=pltpu.CompilerParams(vmem_limit_bytes=20 * MIB),
    )(*scalars, *ins, *after)


def shape(*dims, dtype=BF16):
    return jax.ShapeDtypeStruct(dims, dtype)


def up(ref, lo, hi):
    return ref[lo:hi, :].astype(F32)


def normalize_body(img_ref, txt_ref, img_unit, txt_unit, img_inv, txt_inv, raw_ref, sem):
    copies = [
        pltpu.make_async_copy(src, raw_ref.at[i], sem.at[i])
        for i, src in enumerate((img_ref, txt_ref))
    ]
    for copy in copies:
        copy.start()
    for i, (unit, inv) in enumerate(((img_unit, img_inv), (txt_unit, txt_inv))):
        copies[i].wait()
        v = raw_ref[i].astype(F32)
        r = lax.rsqrt(jnp.sum(v * v, axis=-1, keepdims=True) + EPS)
        unit[...] = (v * r).astype(BF16)
        inv[...] = r


def split3(v):
    hi = v.astype(BF16).astype(F32)
    mid = (v - hi).astype(BF16).astype(F32)
    return hi, mid, v - hi - mid


def loss_rows(total):
    hi, mid, low = split3(total)
    at = lax.broadcasted_iota(jnp.int32, total.shape, 0)
    return jnp.where(at == 0, hi, jnp.where(at == 1, mid, jnp.where(at == 2, low, 0.0))).astype(BF16)


def loss_sum(rows):
    return jnp.sum(rows.astype(F32), axis=0, keepdims=True)


def entry(img, txt, scale, bias, match=None):
    dots = lax.dot_general(img, txt, (((1,), (1,)), ((), ())), preferred_element_type=F32)
    logits = dots * scale + bias
    if match is not None:
        logits = jnp.where(match, -logits, logits)
    e = jnp.exp(logits)
    u = 1.0 + e
    inv = 1.0 / u
    softplus = jnp.log(u) + (e - (u - 1.0)) * inv
    weight = scale * (e * inv)
    if match is not None:
        weight = jnp.where(match, -weight, weight)
    return weight.astype(BF16), softplus


def fold(v):
    total = v[:, :128]
    for n in range(1, v.shape[1] // 128):
        total = total + v[:, 128 * n : 128 * (n + 1)]
    return total


def texts(coeffs, imgs, lo, hi):
    total = None
    for c, s in zip(coeffs, imgs):
        part = lax.dot_general(
            c[:, lo:hi], s[:256, :], (((0,), (0,)), ((), ())), preferred_element_type=F32
        )
        total = part if total is None else total + part
    return total


def tile(img, txt_ref, coeff_ref, total, scale, bias, own=False):
    for lo, hi in ((0, 256), (256, 384)):
        match = None
        if own and lo == 256:
            r = lax.broadcasted_iota(jnp.int32, (256, 128), 0)
            c = lax.broadcasted_iota(jnp.int32, (256, 128), 1)
            match = (r == c) & (r < U)
        weight, softplus = entry(img[:256, :], txt_ref[lo:hi, :], scale, bias, match)
        coeff_ref[:, lo:hi] = weight
        total = total + fold(softplus)
    return total


def near_tile(img, mine_ref, other_ref, coeff_ref, total, scale, bias, own=False):
    weight, softplus = entry(img[:256, :], mine_ref[...], scale, bias)
    coeff_ref[:, :256] = weight
    total = total + fold(softplus)
    return tile(img, other_ref, coeff_ref.at[:, 256:], total, scale, bias, own)


def loss_row(total):
    column = jnp.broadcast_to(jnp.sum(total, axis=1, keepdims=True), (256, 128))
    return jnp.transpose(column)[:8, :]


def near_image(cn, mine, other):
    g = jnp.dot(cn[:, :256], mine[...], preferred_element_type=F32)
    return g + jnp.dot(cn[:, 256:], other[...], preferred_element_type=F32)


def far_image(cf, far):
    return jnp.dot(cf[...], far[...], preferred_element_type=F32)


def mine_body(scale_ref, bias_ref, img_ref, txt_ref, coeff_ref, loss_ref):
    weight, softplus = entry(img_ref[:256, :], txt_ref[...], scale_ref[0], bias_ref[0])
    coeff_ref[...] = weight
    loss_ref[...] = fold(softplus)


def other_body(scale_ref, bias_ref, i0, i1, i3, m0, m1, m3, l0, l1, l3, txt_ref, n0, n1, n3, t0, t1, t3, part):
    groups = ((i0, m0, l0, n0, t0), (i1, m1, l1, n1, t1), (i3, m3, l3, n3, t3))
    for k, (i, m, l, n, t) in enumerate(groups):
        n[:, :256] = m[...]
        t[...] = tile(i, txt_ref, n.at[:, 256:], l[...], scale_ref[0], bias_ref[0], k == 0)
    part[...] = texts((n0, n1, n3), (i0, i1, i3), 0, 640)


def near_images_body(n0, n1, n3, mine, other, g0, g1, g3):
    for n, g in ((n0, g0), (n1, g1), (n3, g3)):
        g[...] = near_image(n, mine, other)


def far_body(scale_ref, bias_ref, i0, i1, i3, far, l0, l1, l3, c0, c1, c3, rows):
    for n, (i, l, c) in enumerate(((i0, l0, c0), (i1, l1, c1), (i3, l3, c3))):
        total = tile(i, far, c, l[...], scale_ref[0], bias_ref[0])
        rows[:, 256 * n : 256 * (n + 1)] = loss_row(total)


def last_body(scale_ref, bias_ref, i0, i1, i2, i3, mine, other, far, c0, c1, c3, part, n2, c2, row, keep_a, send_a, keep_b, send_b, pair):
    scale, bias = scale_ref[0], bias_ref[0]
    total = near_tile(i2, mine, other, n2, jnp.zeros((256, 128), F32), scale, bias)
    row[...] = loss_row(tile(i2, far, c2, total, scale, bias))
    g = texts((c0, c1, c2, c3), (i0, i1, i2, i3), 0, 384)
    keep_a[...] = g[:192, :]
    send_a[...] = g[192:, :].astype(BF16)
    g = part[...] + texts((n2,), (i2,), 0, 640)
    keep_b[...] = g[:256, :]
    send_b[...] = g[256:512, :].astype(BF16)
    pair[...] = g[512:, :]


def send_image(out, g, row):
    out[:256, :] = g.astype(BF16)
    out[256:, :] = jnp.zeros((8, g.shape[1]), BF16)
    out[256:, :256] = loss_rows(row)


def image_body(at, near, cf, far, row, out):
    send_image(out, near[...] + far_image(cf, far), row[:, 256 * at : 256 * (at + 1)])


def last_image_body(cn, cf, mine, other, far, row, out):
    send_image(out, near_image(cn, mine, other) + far_image(cf, far), row[...])


def own_image_body(near, cf, far, out):
    out[...] = near[...] + far_image(cf, far)


def merge_img_body(g_ref, l_ref, r1, r2, r3, own_ref, own_loss, m1, m2, m3):
    loss = l_ref[:, :256] + (
        loss_sum(r1[256:, :256]) + loss_sum(r2[256:, :256]) + loss_sum(r3[256:, :256])
    )
    own_loss[...] = loss
    marks = loss_rows(loss)
    for j, out in enumerate((own_ref, m1, m2, m3)):
        lo, hi = U * j, U * (j + 1)
        total = g_ref[lo:hi, :] + (up(r1, lo, hi) + up(r2, lo, hi) + up(r3, lo, hi))
        out[:U, :] = total.astype(out.dtype)
        if j:
            out[U:, :] = jnp.zeros((8, total.shape[1]), BF16)
            out[U:, :256] = marks


def pack_body(*refs):
    out, at = refs[-1], 0
    for ref in refs[:-1]:
        n = min(ref.shape[0], out.shape[0] - at)
        out[at : at + n, :] = ref[:n, :]
        at += n
    if at < out.shape[0]:
        out[at:, :] = jnp.zeros((out.shape[0] - at, out.shape[1]), out.dtype)


def split_body(b1, b2, half, near):
    half[...] = b2[:U, :]
    near[:128, :] = b2[...]
    near[128:, :] = b1[...]


def step1_body(keep, got, out):
    out[...] = (keep[...] + got[...].astype(F32)).astype(BF16)


def step2_body(keep, got, w, two, one):
    two[:64, :] = (keep[:64, :] + (up(got, 0, 64) + up(w, 0, 64))).astype(BF16)
    two[64:, :] = (keep[64:128, :] + up(got, 64, 128)).astype(BF16)
    one[...] = (keep[128:, :] + (up(got, 128, 256) + up(w, 64, 192))).astype(BF16)


def step3_body(pair, v1, v2, out):
    out[...] = (pair[64:, :] + (up(v1, 64, 128) + up(v2, 64, 128))).astype(BF16)


def back_norm(g, raw, inv):
    unit = raw[...].astype(F32) * inv[...]
    return inv[...] * (g - unit * jnp.sum(unit * g, axis=-1, keepdims=True))


def finish_body(g_ref, l_ref, r1, r2, r3, raw_i, inv_i, pair, v1, v2, got, raw_t, inv_t, img_ref, txt_ref, loss_ref):
    g = g_ref[...] + (up(r1, 0, U) + up(r2, 0, U) + up(r3, 0, U))
    img_ref[...] = back_norm(g, raw_i, inv_i)
    loss = l_ref[:1, :U]
    for j, r in enumerate((r1, r2, r3)):
        loss = loss + loss_sum(r[U:, U * (j + 1) : U * (j + 2)])
    loss_ref[...] = loss
    g = pair[:64, :] + (up(v1, 0, 64) + up(v2, 0, 64) + got[...].astype(F32))
    txt_ref[...] = back_norm(g, raw_t, inv_t)


def on_device(picture, caption, scale, bias):
    rows, d = picture.shape
    img, txt, img_inv, txt_inv = call(
        "normalize", normalize_body,
        [shape(rows, d), shape(rows, d), shape(rows, 1, dtype=F32), shape(rows, 1, dtype=F32)],
        [pltpu.with_memory_space_constraint(a, pltpu.HBM) for a in (picture, caption)], specs=[HBM] * 2,
        scratch=[pltpu.VMEM((2, rows, d), BF16), pltpu.SemaphoreType.DMA((2,))],
    )

    def pack(name, n, parts, after=()):
        return call(name, pack_body, [shape(n, d)], parts, (), after)[0]

    pair = pack("pair", 128, (txt, swap(txt)))
    b2, b1 = ring(pair, 2), ring(pair, 1)
    f2, f1, f3 = first(img, 2), first(img, 1), first(img, 3)
    group = pack("group", 264, (img, f1, f2, f3))
    g1, g3, g2 = second(group, 1), second(group, 3), second(group, 2)
    groups = (group, g1, g2, g3)
    half, near_mine = call(
        "pack", split_body, [shape(64, d), shape(256, d)], (b1, b2), (), (group,)
    )
    near_other = swap(near_mine)
    b3, b4 = ring(b2, 1), ring(half, 2)

    sc = (scale, bias)
    mine_c, mine_l, last = {}, {}, ()
    for k in (0, 1, 3):
        mine_c[k], mine_l[k] = call(
            f"mine{k}", mine_body, [shape(256, 256), shape(256, 128, dtype=F32)],
            (groups[k], near_mine), sc, last,
        )
        last = (mine_l[k],)
    other = pack("other_texts", 384, (near_other, pair), last)
    n0, n1, n3, l0, l1, l3, part = call(
        "other", other_body,
        [shape(256, 640)] * 3 + [shape(256, 128, dtype=F32)] * 3 + [shape(640, d, dtype=F32)],
        (group, g1, g3, *mine_c.values(), *mine_l.values(), other), sc,
    )
    far_mine = pack("far_mine", 192, (b4, b3), (l0,))
    far_other = swap(far_mine)
    t0, t1, t3 = call(
        "near_images", near_images_body, [shape(256, d, dtype=F32)] * 3,
        (n0, n1, n3, near_mine, other), (), (far_mine,),
    )
    far = pack("far_texts", 384, (far_mine, far_other), (t0,))
    c0, c1, c3, rows013 = call(
        "far", far_body, [shape(256, 384)] * 3 + [shape(8, 768, dtype=F32)],
        (group, g1, g3, far, l0, l1, l3), sc,
    )
    n2, c2, row2, keep_a, send_a, keep_b, send_b, own_pair = call(
        "last", last_body,
        [shape(256, 640), shape(256, 384), shape(8, 256, dtype=F32)]
        + [shape(192, d, dtype=F32), shape(192, d), shape(256, d, dtype=F32), shape(256, d), shape(128, d, dtype=F32)],
        (*groups, near_mine, other, far, c0, c1, c3, part), sc,
    )
    got_a, got_b = swap(send_a), swap(send_b)

    def sent(name, at, near, cf, after):
        return call(
            name, functools.partial(image_body, at), [shape(264, d)],
            (near, cf, far, rows013), (), after,
        )[0]

    p1 = sent("image1", 1, t1, c1, (send_a,))
    p3 = sent("image3", 2, t3, c3, (p1,))
    p2 = call(
        "image2", last_image_body, [shape(264, d)], (n2, c2, near_mine, other, far, row2), (), (p3,)
    )[0]
    z1 = call("step1", step1_body, [shape(192, d)], (keep_a, got_a), (), (p2, got_b))[0]
    w = ring(z1, -2)
    r1, r3, r2 = second(p1, -1), second(p3, -3), second(p2, -2)
    p0 = call(
        "own_image", own_image_body, [shape(256, d, dtype=F32)], (t0, c0, far), (), (z1,)
    )[0]
    two, one = call("step2", step2_body, [shape(128, d)] * 2, (keep_b, got_b, w), (), (p0,))
    v2, v1 = ring(two, -2), ring(one, -1)
    own_img, own_loss, m1, m2, m3 = call(
        "merge_img", merge_img_body,
        [shape(rows, d, dtype=F32), shape(8, 256, dtype=F32)] + [shape(rows + 8, d)] * 3,
        (p0, rows013, r1, r2, r3), (), (one,),
    )
    q1, q3, q2 = first(m1, -1), first(m3, -3), first(m2, -2)
    z3 = call("step3", step3_body, [shape(64, d)], (own_pair, v1, v2), (), (m3,))[0]
    got_c = swap(z3)
    grad_img, grad_txt, loss_out = call(
        "finish", finish_body,
        [shape(rows, d, dtype=F32), shape(rows, d, dtype=F32), shape(1, rows, dtype=F32)],
        (own_img, own_loss, q1, q2, q3, picture, img_inv, own_pair, v1, v2, got_c, caption, txt_inv),
    )
    return grad_img, grad_txt, loss_out.reshape(rows)


def solution(mesh):
    torus = Mesh(mesh.devices.reshape(NX, NC, NZ, NY), AXES)
    return jax.shard_map(
        on_device,
        mesh=torus,
        in_specs=(P(AXES, None), P(AXES, None), P(), P()),
        out_specs=(P(AXES, None), P(AXES, None), P(AXES)),
        check_vma=False,
    )
```

```python
import functools

import jax
import jax.numpy as jnp
from jax import lax
from jax.experimental import pallas as pl
from jax.experimental.pallas import tpu as pltpu
from jax.sharding import Mesh
from jax.sharding import PartitionSpec as P

AXES = ("x", "core", "z", "y")
NX, NC, NZ, NY = 4, 2, 8, 4
U = 64
EPS = 1e-06
F32 = jnp.float32
BF16 = jnp.bfloat16
MIB = 1 << 20
VMEM = pl.BlockSpec(memory_space=pltpu.VMEM)
SMEM = pl.BlockSpec(memory_space=pltpu.SMEM)
ANY = pl.BlockSpec(memory_space=pl.ANY)
HBM = pl.BlockSpec(memory_space=pltpu.HBM)


def device(x, core, z, y):
    return ((x % NX * NC + core) * NZ + z % NZ) * NY + y % NY


def permutation(move):
    return [
        (device(x, c, z, y), device(*move(x, c, z, y)))
        for x in range(NX)
        for c in range(NC)
        for z in range(NZ)
        for y in range(NY)
    ]


def first(a, s):
    return lax.ppermute(
        a, AXES, permutation(lambda x, c, z, y: (x, c, z, y + s) if c else (x + s, c, z, y))
    )


def second(a, s):
    return lax.ppermute(
        a, AXES, permutation(lambda x, c, z, y: (x + s, c, z, y) if c else (x, c, z, y + s))
    )


def ring(a, s):
    return lax.ppermute(a, AXES, permutation(lambda x, c, z, y: (x, c, z - s if c else z + s, y)))


def swap(a):
    return lax.ppermute(a, AXES, permutation(lambda x, c, z, y: (x, 1 - c, z, y)))


def call(name, body, outs, ins, scalars=(), after=(), specs=None, scratch=()):
    n_out, n_in = len(outs), len(ins) + len(scalars)

    def kernel(*refs):
        used = refs[:n_in] + refs[n_in + len(after) :]
        body(*used)

    return pl.pallas_call(
        kernel,
        out_shape=outs,
        in_specs=[SMEM] * len(scalars) + (specs or [VMEM] * len(ins)) + [ANY] * len(after),
        out_specs=[VMEM] * n_out,
        scratch_shapes=list(scratch),
        name=name,
        cost_estimate=pl.CostEstimate(flops=1, bytes_accessed=1, transcendentals=0),
        compiler_params=pltpu.CompilerParams(vmem_limit_bytes=20 * MIB),
    )(*scalars, *ins, *after)


def shape(*dims, dtype=BF16):
    return jax.ShapeDtypeStruct(dims, dtype)


def up(ref, lo, hi):
    return ref[lo:hi, :].astype(F32)


def normalize_body(img_ref, txt_ref, img_unit, txt_unit, img_inv, txt_inv, raw_ref, sem):
    copies = [
        pltpu.make_async_copy(src, raw_ref.at[i], sem.at[i])
        for i, src in enumerate((img_ref, txt_ref))
    ]
    for copy in copies:
        copy.start()
    for i, (unit, inv) in enumerate(((img_unit, img_inv), (txt_unit, txt_inv))):
        copies[i].wait()
        v = raw_ref[i].astype(F32)
        r = lax.rsqrt(jnp.sum(v * v, axis=-1, keepdims=True) + EPS)
        unit[...] = (v * r).astype(BF16)
        inv[...] = r


def split3(v):
    hi = v.astype(BF16).astype(F32)
    mid = (v - hi).astype(BF16).astype(F32)
    return hi, mid, v - hi - mid


def loss_rows(total):
    hi, mid, low = split3(total)
    at = lax.broadcasted_iota(jnp.int32, total.shape, 0)
    return jnp.where(at == 0, hi, jnp.where(at == 1, mid, jnp.where(at == 2, low, 0.0))).astype(BF16)


def loss_sum(rows):
    return jnp.sum(rows.astype(F32), axis=0, keepdims=True)


def entry(img, txt, scale, bias, match=None):
    dots = lax.dot_general(img, txt, (((1,), (1,)), ((), ())), preferred_element_type=F32)
    logits = dots * scale + bias
    if match is not None:
        logits = jnp.where(match, -logits, logits)
    e = jnp.exp(logits)
    u = 1.0 + e
    inv = 1.0 / u
    softplus = jnp.log(u) + (e - (u - 1.0)) * inv
    weight = scale * (e * inv)
    if match is not None:
        weight = jnp.where(match, -weight, weight)
    return weight.astype(BF16), softplus


def fold(v):
    total = v[:, :128]
    for n in range(1, v.shape[1] // 128):
        total = total + v[:, 128 * n : 128 * (n + 1)]
    return total


def texts(coeffs, imgs, lo, hi):
    total = None
    for c, s in zip(coeffs, imgs):
        part = lax.dot_general(
            c[:, lo:hi], s[:256, :], (((0,), (0,)), ((), ())), preferred_element_type=F32
        )
        total = part if total is None else total + part
    return total


def tile(img, txt_ref, coeff_ref, total, scale, bias, own=False):
    for lo, hi in ((0, 256), (256, 384)):
        match = None
        if own and lo == 256:
            r = lax.broadcasted_iota(jnp.int32, (256, 128), 0)
            c = lax.broadcasted_iota(jnp.int32, (256, 128), 1)
            match = (r == c) & (r < U)
        weight, softplus = entry(img[:256, :], txt_ref[lo:hi, :], scale, bias, match)
        coeff_ref[:, lo:hi] = weight
        total = total + fold(softplus)
    return total


def near_tile(img, mine_ref, other_ref, coeff_ref, total, scale, bias, own=False):
    weight, softplus = entry(img[:256, :], mine_ref[...], scale, bias)
    coeff_ref[:, :256] = weight
    total = total + fold(softplus)
    return tile(img, other_ref, coeff_ref.at[:, 256:], total, scale, bias, own)


def loss_row(total):
    column = jnp.broadcast_to(jnp.sum(total, axis=1, keepdims=True), (256, 128))
    return jnp.transpose(column)[:8, :]


def near_image(cn, mine, other):
    g = jnp.dot(cn[:, :256], mine[...], preferred_element_type=F32)
    return g + jnp.dot(cn[:, 256:], other[...], preferred_element_type=F32)


def far_image(cf, far):
    return jnp.dot(cf[...], far[...], preferred_element_type=F32)


def mine_body(scale_ref, bias_ref, img_ref, txt_ref, coeff_ref, loss_ref):
    weight, softplus = entry(img_ref[:256, :], txt_ref[...], scale_ref[0], bias_ref[0])
    coeff_ref[...] = weight
    loss_ref[...] = fold(softplus)


def other_body(scale_ref, bias_ref, i0, i1, i3, m0, m1, m3, l0, l1, l3, mine, txt_ref, n1, n3, t0, t1, t3, part, g0, n0):
    groups = ((i0, m0, l0, n0, t0), (i1, m1, l1, n1, t1), (i3, m3, l3, n3, t3))
    for k, (i, m, l, n, t) in enumerate(groups):
        n[:, :256] = m[...]
        t[...] = tile(i, txt_ref, n.at[:, 256:], l[...], scale_ref[0], bias_ref[0], k == 0)
    part[...] = texts((n0, n1, n3), (i0, i1, i3), 0, 640)
    g0[...] = near_image(n0, mine, txt_ref)


def near_images_body(n1, n3, mine, other, g1, g3):
    for n, g in ((n1, g1), (n3, g3)):
        g[...] = near_image(n, mine, other)


def far_body(scale_ref, bias_ref, i0, i1, i3, far, l0, l1, l3, c0, c1, c3, rows):
    for n, (i, l, c) in enumerate(((i0, l0, c0), (i1, l1, c1), (i3, l3, c3))):
        total = tile(i, far, c, l[...], scale_ref[0], bias_ref[0])
        rows[:, 256 * n : 256 * (n + 1)] = loss_row(total)


def last_body(scale_ref, bias_ref, i0, i1, i2, i3, mine, other, far, c0, c1, c3, part, n2, c2, row, keep_a, send_a, keep_b, send_b, pair):
    scale, bias = scale_ref[0], bias_ref[0]
    total = near_tile(i2, mine, other, n2, jnp.zeros((256, 128), F32), scale, bias)
    row[...] = loss_row(tile(i2, far, c2, total, scale, bias))
    g = texts((c0, c1, c2, c3), (i0, i1, i2, i3), 0, 384)
    keep_a[...] = g[:192, :]
    send_a[...] = g[192:, :].astype(BF16)
    g = part[...] + texts((n2,), (i2,), 0, 640)
    keep_b[...] = g[:256, :]
    send_b[...] = g[256:512, :].astype(BF16)
    pair[...] = g[512:, :]


def send_image(out, g, row):
    out[:256, :] = g.astype(BF16)
    out[256:, :] = jnp.zeros((8, g.shape[1]), BF16)
    out[256:, :256] = loss_rows(row)


def image_body(at, near, cf, far, row, out):
    send_image(out, near[...] + far_image(cf, far), row[:, 256 * at : 256 * (at + 1)])


def last_image_body(cn, cf, mine, other, far, row, out):
    send_image(out, near_image(cn, mine, other) + far_image(cf, far), row[...])


def own_image_body(near, cf, far, out):
    out[...] = near[...] + far_image(cf, far)


def merge_img_body(g_ref, l_ref, r1, r2, r3, own_ref, own_loss, m1, m2, m3):
    loss = l_ref[:, :256] + (
        loss_sum(r1[256:, :256]) + loss_sum(r2[256:, :256]) + loss_sum(r3[256:, :256])
    )
    own_loss[...] = loss
    marks = loss_rows(loss)
    for j, out in enumerate((own_ref, m1, m2, m3)):
        lo, hi = U * j, U * (j + 1)
        total = g_ref[lo:hi, :] + (up(r1, lo, hi) + up(r2, lo, hi) + up(r3, lo, hi))
        out[:U, :] = total.astype(out.dtype)
        if j:
            out[U:, :] = jnp.zeros((8, total.shape[1]), BF16)
            out[U:, :256] = marks


def pack_body(*refs):
    out, at = refs[-1], 0
    for ref in refs[:-1]:
        n = min(ref.shape[0], out.shape[0] - at)
        out[at : at + n, :] = ref[:n, :]
        at += n
    if at < out.shape[0]:
        out[at:, :] = jnp.zeros((out.shape[0] - at, out.shape[1]), out.dtype)


def split_body(b1, b2, half, near):
    half[...] = b2[:U, :]
    near[:128, :] = b2[...]
    near[128:, :] = b1[...]


def step1_body(keep, got, out):
    out[...] = (keep[...] + got[...].astype(F32)).astype(BF16)


def step2_body(keep, got, w, two, one):
    two[:64, :] = (keep[:64, :] + (up(got, 0, 64) + up(w, 0, 64))).astype(BF16)
    two[64:, :] = (keep[64:128, :] + up(got, 64, 128)).astype(BF16)
    one[...] = (keep[128:, :] + (up(got, 128, 256) + up(w, 64, 192))).astype(BF16)


def step3_body(pair, v1, v2, out):
    out[...] = (pair[64:, :] + (up(v1, 64, 128) + up(v2, 64, 128))).astype(BF16)


def back_norm(g, raw, inv):
    unit = raw[...].astype(F32) * inv[...]
    return inv[...] * (g - unit * jnp.sum(unit * g, axis=-1, keepdims=True))


def finish_body(g_ref, l_ref, r1, r2, r3, raw_i, inv_i, pair, v1, v2, got, raw_t, inv_t, img_ref, txt_ref, loss_ref):
    g = g_ref[...] + (up(r1, 0, U) + up(r2, 0, U) + up(r3, 0, U))
    img_ref[...] = back_norm(g, raw_i, inv_i)
    loss = l_ref[:1, :U]
    for j, r in enumerate((r1, r2, r3)):
        loss = loss + loss_sum(r[U:, U * (j + 1) : U * (j + 2)])
    loss_ref[...] = loss
    g = pair[:64, :] + (up(v1, 0, 64) + up(v2, 0, 64) + got[...].astype(F32))
    txt_ref[...] = back_norm(g, raw_t, inv_t)


def on_device(picture, caption, scale, bias):
    rows, d = picture.shape
    img, txt, img_inv, txt_inv = call(
        "normalize", normalize_body,
        [shape(rows, d), shape(rows, d), shape(rows, 1, dtype=F32), shape(rows, 1, dtype=F32)],
        [pltpu.with_memory_space_constraint(a, pltpu.HBM) for a in (picture, caption)], specs=[HBM] * 2,
        scratch=[pltpu.VMEM((2, rows, d), BF16), pltpu.SemaphoreType.DMA((2,))],
    )

    def pack(name, n, parts, after=()):
        return call(name, pack_body, [shape(n, d)], parts, (), after)[0]

    pair = pack("pair", 128, (txt, swap(txt)))
    b1, b2 = ring(pair, 1), ring(pair, 2)
    f1, f3, f2 = first(img, 1), first(img, 3), first(img, 2)
    group = pack("group", 264, (img, f1, f2, f3))
    g1, g3, g2 = second(group, 1), second(group, 3), second(group, 2)
    groups = (group, g1, g2, g3)
    half, near_mine = call(
        "pack", split_body, [shape(64, d), shape(256, d)], (b1, b2), (), (group,)
    )
    near_other = swap(near_mine)
    b3, b4 = ring(b2, 1), ring(half, 2)

    sc = (scale, bias)
    mine_c, mine_l, last = {}, {}, ()
    for k in (0, 1, 3):
        mine_c[k], mine_l[k] = call(
            f"mine{k}", mine_body, [shape(256, 256), shape(256, 128, dtype=F32)],
            (groups[k], near_mine), sc, last,
        )
        last = (mine_l[k],)
    other = pack("other_texts", 384, (near_other, pair), last)
    n1, n3, l0, l1, l3, part, t0 = call(
        "other", other_body,
        [shape(256, 640)] * 2 + [shape(256, 128, dtype=F32)] * 3
        + [shape(640, d, dtype=F32), shape(256, d, dtype=F32)],
        (group, g1, g3, *mine_c.values(), *mine_l.values(), near_mine, other), sc,
        scratch=[pltpu.VMEM((256, 640), BF16)],
    )
    far_mine = pack("far_mine", 192, (b4, b3), (l0,))
    far_other = swap(far_mine)
    t1, t3 = call(
        "near_images", near_images_body, [shape(256, d, dtype=F32)] * 2,
        (n1, n3, near_mine, other), (), (far_mine,),
    )
    far = pack("far_texts", 384, (far_mine, far_other), (t1,))
    c0, c1, c3, rows013 = call(
        "far", far_body, [shape(256, 384)] * 3 + [shape(8, 768, dtype=F32)],
        (group, g1, g3, far, l0, l1, l3), sc,
    )
    n2, c2, row2, keep_a, send_a, keep_b, send_b, own_pair = call(
        "last", last_body,
        [shape(256, 640), shape(256, 384), shape(8, 256, dtype=F32)]
        + [shape(192, d, dtype=F32), shape(192, d), shape(256, d, dtype=F32), shape(256, d), shape(128, d, dtype=F32)],
        (*groups, near_mine, other, far, c0, c1, c3, part), sc,
    )
    got_a, got_b = swap(send_a), swap(send_b)

    def sent(name, at, near, cf, after):
        return call(
            name, functools.partial(image_body, at), [shape(264, d)],
            (near, cf, far, rows013), (), after,
        )[0]

    p1 = sent("image1", 1, t1, c1, (send_a,))
    p3 = sent("image3", 2, t3, c3, (p1,))
    p2 = call(
        "image2", last_image_body, [shape(264, d)], (n2, c2, near_mine, other, far, row2), (), (p3,)
    )[0]
    z1 = call("step1", step1_body, [shape(192, d)], (keep_a, got_a), (), (p2, got_b))[0]
    w = ring(z1, -2)
    r1, r3, r2 = second(p1, -1), second(p3, -3), second(p2, -2)
    p0 = call(
        "own_image", own_image_body, [shape(256, d, dtype=F32)], (t0, c0, far), (), (z1,)
    )[0]
    two, one = call("step2", step2_body, [shape(128, d)] * 2, (keep_b, got_b, w), (), (p0,))
    v2, v1 = ring(two, -2), ring(one, -1)
    own_img, own_loss, m1, m2, m3 = call(
        "merge_img", merge_img_body,
        [shape(rows, d, dtype=F32), shape(8, 256, dtype=F32)] + [shape(rows + 8, d)] * 3,
        (p0, rows013, r1, r2, r3), (), (one,),
    )
    q1, q3, q2 = first(m1, -1), first(m3, -3), first(m2, -2)
    z3 = call("step3", step3_body, [shape(64, d)], (own_pair, v1, v2), (), (m3,))[0]
    got_c = swap(z3)
    grad_img, grad_txt, loss_out = call(
        "finish", finish_body,
        [shape(rows, d, dtype=F32), shape(rows, d, dtype=F32), shape(1, rows, dtype=F32)],
        (own_img, own_loss, q1, q2, q3, picture, img_inv, own_pair, v1, v2, got_c, caption, txt_inv),
    )
    return grad_img, grad_txt, loss_out.reshape(rows)


def solution(mesh):
    torus = Mesh(mesh.devices.reshape(NX, NC, NZ, NY), AXES)
    return jax.shard_map(
        on_device,
        mesh=torus,
        in_specs=(P(AXES, None), P(AXES, None), P(), P()),
        out_specs=(P(AXES, None), P(AXES, None), P(AXES)),
        check_vma=False,
    )
```

```python
import functools

import jax
import jax.numpy as jnp
from jax import lax
from jax.experimental import pallas as pl
from jax.experimental.pallas import tpu as pltpu
from jax.sharding import Mesh
from jax.sharding import PartitionSpec as P

AXES = ("x", "core", "z", "y")
NX, NC, NZ, NY = 4, 2, 8, 4
U = 64
EPS = 1e-06
LOG2E = 1.4426950408889634
F32 = jnp.float32
BF16 = jnp.bfloat16
MIB = 1 << 20
VMEM = pl.BlockSpec(memory_space=pltpu.VMEM)
SMEM = pl.BlockSpec(memory_space=pltpu.SMEM)
ANY = pl.BlockSpec(memory_space=pl.ANY)
HBM = pl.BlockSpec(memory_space=pltpu.HBM)


def device(x, core, z, y):
    return ((x % NX * NC + core) * NZ + z % NZ) * NY + y % NY


def permutation(move):
    return [
        (device(x, c, z, y), device(*move(x, c, z, y)))
        for x in range(NX)
        for c in range(NC)
        for z in range(NZ)
        for y in range(NY)
    ]


def first(a, s):
    return lax.ppermute(
        a, AXES, permutation(lambda x, c, z, y: (x, c, z, y + s) if c else (x + s, c, z, y))
    )


def second(a, s):
    return lax.ppermute(
        a, AXES, permutation(lambda x, c, z, y: (x + s, c, z, y) if c else (x, c, z, y + s))
    )


def ring(a, s):
    return lax.ppermute(a, AXES, permutation(lambda x, c, z, y: (x, c, z - s if c else z + s, y)))


def swap(a):
    return lax.ppermute(a, AXES, permutation(lambda x, c, z, y: (x, 1 - c, z, y)))


def call(name, body, outs, ins, scalars=(), after=(), specs=None, scratch=()):
    n_out, n_in = len(outs), len(ins) + len(scalars)

    def kernel(*refs):
        used = refs[:n_in] + refs[n_in + len(after) :]
        body(*used)

    return pl.pallas_call(
        kernel,
        out_shape=outs,
        in_specs=[SMEM] * len(scalars) + (specs or [VMEM] * len(ins)) + [ANY] * len(after),
        out_specs=[VMEM] * n_out,
        scratch_shapes=list(scratch),
        name=name,
        cost_estimate=pl.CostEstimate(flops=1, bytes_accessed=1, transcendentals=0),
        compiler_params=pltpu.CompilerParams(vmem_limit_bytes=20 * MIB),
    )(*scalars, *ins, *after)


def shape(*dims, dtype=BF16):
    return jax.ShapeDtypeStruct(dims, dtype)


def up(ref, lo, hi):
    return ref[lo:hi, :].astype(F32)


def normalize_body(img_ref, txt_ref, img_unit, txt_unit, img_inv, txt_inv, raw_ref, sem):
    copies = [
        pltpu.make_async_copy(src, raw_ref.at[i], sem.at[i])
        for i, src in enumerate((img_ref, txt_ref))
    ]
    for copy in copies:
        copy.start()
    for i, (unit, inv) in enumerate(((img_unit, img_inv), (txt_unit, txt_inv))):
        copies[i].wait()
        v = raw_ref[i].astype(F32)
        r = lax.rsqrt(jnp.sum(v * v, axis=-1, keepdims=True) + EPS)
        unit[...] = (v * r).astype(BF16)
        inv[...] = r


def split3(v):
    hi = v.astype(BF16).astype(F32)
    mid = (v - hi).astype(BF16).astype(F32)
    return hi, mid, v - hi - mid


def loss_rows(total):
    hi, mid, low = split3(total)
    at = lax.broadcasted_iota(jnp.int32, total.shape, 0)
    return jnp.where(at == 0, hi, jnp.where(at == 1, mid, jnp.where(at == 2, low, 0.0))).astype(BF16)


def loss_sum(rows):
    return jnp.sum(rows.astype(F32), axis=0, keepdims=True)


def entry(img, txt, scale, bias, match=None):
    dots = lax.dot_general(img, txt, (((1,), (1,)), ((), ())), preferred_element_type=F32)
    logits = dots * (scale * LOG2E) + bias * LOG2E
    if match is not None:
        logits = jnp.where(match, -logits, logits)
    e = jnp.exp2(logits)
    u = 1.0 + e
    inv = 1.0 / u
    softplus = jnp.log(u) + (e - (u - 1.0)) * inv
    weight = scale * (e * inv)
    if match is not None:
        weight = jnp.where(match, -weight, weight)
    return weight.astype(BF16), softplus


def fold(v):
    total = v[:, :128]
    for n in range(1, v.shape[1] // 128):
        total = total + v[:, 128 * n : 128 * (n + 1)]
    return total


def texts(coeffs, imgs, lo, hi):
    total = None
    for c, s in zip(coeffs, imgs):
        part = lax.dot_general(
            c[:, lo:hi], s[:256, :], (((0,), (0,)), ((), ())), preferred_element_type=F32
        )
        total = part if total is None else total + part
    return total


def tile(img, txt_ref, coeff_ref, total, scale, bias, own=False):
    for lo, hi in ((0, 256), (256, 384)):
        match = None
        if own and lo == 256:
            r = lax.broadcasted_iota(jnp.int32, (256, 128), 0)
            c = lax.broadcasted_iota(jnp.int32, (256, 128), 1)
            match = (r == c) & (r < U)
        weight, softplus = entry(img[:256, :], txt_ref[lo:hi, :], scale, bias, match)
        coeff_ref[:, lo:hi] = weight
        total = total + fold(softplus)
    return total


def near_tile(img, mine_ref, other_ref, coeff_ref, total, scale, bias, own=False):
    weight, softplus = entry(img[:256, :], mine_ref[...], scale, bias)
    coeff_ref[:, :256] = weight
    total = total + fold(softplus)
    return tile(img, other_ref, coeff_ref.at[:, 256:], total, scale, bias, own)


def loss_row(total):
    column = jnp.broadcast_to(jnp.sum(total, axis=1, keepdims=True), (256, 128))
    return jnp.transpose(column)[:8, :]


def near_image(cn, mine, other):
    g = jnp.dot(cn[:, :256], mine[...], preferred_element_type=F32)
    return g + jnp.dot(cn[:, 256:], other[...], preferred_element_type=F32)


def far_image(cf, far):
    return jnp.dot(cf[...], far[...], preferred_element_type=F32)


def mine_body(scale_ref, bias_ref, img_ref, txt_ref, coeff_ref, loss_ref):
    weight, softplus = entry(img_ref[:256, :], txt_ref[...], scale_ref[0], bias_ref[0])
    coeff_ref[...] = weight
    loss_ref[...] = fold(softplus)


def other_body(scale_ref, bias_ref, i0, i1, i3, m0, m1, m3, l0, l1, l3, mine, txt_ref, n1, n3, t0, t1, t3, part, g0, n0):
    groups = ((i0, m0, l0, n0, t0), (i1, m1, l1, n1, t1), (i3, m3, l3, n3, t3))
    for k, (i, m, l, n, t) in enumerate(groups):
        n[:, :256] = m[...]
        t[...] = tile(i, txt_ref, n.at[:, 256:], l[...], scale_ref[0], bias_ref[0], k == 0)
    part[...] = texts((n0, n1, n3), (i0, i1, i3), 0, 640)
    g0[...] = near_image(n0, mine, txt_ref)


def near_images_body(n1, n3, mine, other, g1, g3):
    for n, g in ((n1, g1), (n3, g3)):
        g[...] = near_image(n, mine, other)


def far_body(scale_ref, bias_ref, i0, i1, i3, far, l0, l1, l3, c0, c1, c3, rows):
    for n, (i, l, c) in enumerate(((i0, l0, c0), (i1, l1, c1), (i3, l3, c3))):
        total = tile(i, far, c, l[...], scale_ref[0], bias_ref[0])
        rows[:, 256 * n : 256 * (n + 1)] = loss_row(total)


def last_body(scale_ref, bias_ref, i0, i1, i2, i3, mine, other, far, c0, c1, c3, part, n2, c2, row, keep_a, send_a, keep_b, send_b, pair):
    scale, bias = scale_ref[0], bias_ref[0]
    total = near_tile(i2, mine, other, n2, jnp.zeros((256, 128), F32), scale, bias)
    row[...] = loss_row(tile(i2, far, c2, total, scale, bias))
    g = texts((c0, c1, c2, c3), (i0, i1, i2, i3), 0, 384)
    keep_a[...] = g[:192, :]
    send_a[...] = g[192:, :].astype(BF16)
    g = part[...] + texts((n2,), (i2,), 0, 640)
    keep_b[...] = g[:256, :]
    send_b[...] = g[256:512, :].astype(BF16)
    pair[...] = g[512:, :]


def send_image(out, g, row):
    out[:256, :] = g.astype(BF16)
    out[256:, :] = jnp.zeros((8, g.shape[1]), BF16)
    out[256:, :256] = loss_rows(row)


def image_body(at, near, cf, far, row, out):
    send_image(out, near[...] + far_image(cf, far), row[:, 256 * at : 256 * (at + 1)])


def last_image_body(cn, cf, mine, other, far, row, out):
    send_image(out, near_image(cn, mine, other) + far_image(cf, far), row[...])


def own_image_body(near, cf, far, out):
    out[...] = near[...] + far_image(cf, far)


def merge_img_body(g_ref, l_ref, r1, r2, r3, own_ref, own_loss, m1, m2, m3):
    loss = l_ref[:, :256] + (
        loss_sum(r1[256:, :256]) + loss_sum(r2[256:, :256]) + loss_sum(r3[256:, :256])
    )
    own_loss[...] = loss
    marks = loss_rows(loss)
    for j, out in enumerate((own_ref, m1, m2, m3)):
        lo, hi = U * j, U * (j + 1)
        total = g_ref[lo:hi, :] + (up(r1, lo, hi) + up(r2, lo, hi) + up(r3, lo, hi))
        out[:U, :] = total.astype(out.dtype)
        if j:
            out[U:, :] = jnp.zeros((8, total.shape[1]), BF16)
            out[U:, :256] = marks


def pack_body(*refs):
    out, at = refs[-1], 0
    for ref in refs[:-1]:
        n = min(ref.shape[0], out.shape[0] - at)
        out[at : at + n, :] = ref[:n, :]
        at += n
    if at < out.shape[0]:
        out[at:, :] = jnp.zeros((out.shape[0] - at, out.shape[1]), out.dtype)


def split_body(b1, b2, half, near):
    half[...] = b2[:U, :]
    near[:128, :] = b2[...]
    near[128:, :] = b1[...]


def step1_body(keep, got, out):
    out[...] = (keep[...] + got[...].astype(F32)).astype(BF16)


def step2_body(keep, got, w, two, one):
    two[:64, :] = (keep[:64, :] + (up(got, 0, 64) + up(w, 0, 64))).astype(BF16)
    two[64:, :] = (keep[64:128, :] + up(got, 64, 128)).astype(BF16)
    one[...] = (keep[128:, :] + (up(got, 128, 256) + up(w, 64, 192))).astype(BF16)


def step3_body(pair, v1, v2, out):
    out[...] = (pair[64:, :] + (up(v1, 64, 128) + up(v2, 64, 128))).astype(BF16)


def back_norm(g, raw, inv):
    unit = raw[...].astype(F32) * inv[...]
    return inv[...] * (g - unit * jnp.sum(unit * g, axis=-1, keepdims=True))


def finish_body(g_ref, l_ref, r1, r2, r3, raw_i, inv_i, pair, v1, v2, got, raw_t, inv_t, img_ref, txt_ref, loss_ref):
    g = g_ref[...] + (up(r1, 0, U) + up(r2, 0, U) + up(r3, 0, U))
    img_ref[...] = back_norm(g, raw_i, inv_i)
    loss = l_ref[:1, :U]
    for j, r in enumerate((r1, r2, r3)):
        loss = loss + loss_sum(r[U:, U * (j + 1) : U * (j + 2)])
    loss_ref[...] = loss
    g = pair[:64, :] + (up(v1, 0, 64) + up(v2, 0, 64) + got[...].astype(F32))
    txt_ref[...] = back_norm(g, raw_t, inv_t)


def on_device(picture, caption, scale, bias):
    rows, d = picture.shape
    img, txt, img_inv, txt_inv = call(
        "normalize", normalize_body,
        [shape(rows, d), shape(rows, d), shape(rows, 1, dtype=F32), shape(rows, 1, dtype=F32)],
        [pltpu.with_memory_space_constraint(a, pltpu.HBM) for a in (picture, caption)], specs=[HBM] * 2,
        scratch=[pltpu.VMEM((2, rows, d), BF16), pltpu.SemaphoreType.DMA((2,))],
    )

    def pack(name, n, parts, after=()):
        return call(name, pack_body, [shape(n, d)], parts, (), after)[0]

    pair = pack("pair", 128, (txt, swap(txt)))
    b1, b2 = ring(pair, 1), ring(pair, 2)
    f1, f3, f2 = first(img, 1), first(img, 3), first(img, 2)
    group = pack("group", 264, (img, f1, f2, f3))
    g1, g3, g2 = second(group, 1), second(group, 3), second(group, 2)
    groups = (group, g1, g2, g3)
    half, near_mine = call(
        "pack", split_body, [shape(64, d), shape(256, d)], (b1, b2), (), (group,)
    )
    near_other = swap(near_mine)
    b3, b4 = ring(b2, 1), ring(half, 2)

    sc = (scale, bias)
    mine_c, mine_l, last = {}, {}, ()
    for k in (0, 1, 3):
        mine_c[k], mine_l[k] = call(
            f"mine{k}", mine_body, [shape(256, 256), shape(256, 128, dtype=F32)],
            (groups[k], near_mine), sc, last,
        )
        last = (mine_l[k],)
    other = pack("other_texts", 384, (near_other, pair), last)
    n1, n3, l0, l1, l3, part, t0 = call(
        "other", other_body,
        [shape(256, 640)] * 2 + [shape(256, 128, dtype=F32)] * 3
        + [shape(640, d, dtype=F32), shape(256, d, dtype=F32)],
        (group, g1, g3, *mine_c.values(), *mine_l.values(), near_mine, other), sc,
        scratch=[pltpu.VMEM((256, 640), BF16)],
    )
    far_mine = pack("far_mine", 192, (b4, b3), (l0,))
    far_other = swap(far_mine)
    t1, t3 = call(
        "near_images", near_images_body, [shape(256, d, dtype=F32)] * 2,
        (n1, n3, near_mine, other), (), (far_mine,),
    )
    far = pack("far_texts", 384, (far_mine, far_other), (t1,))
    c0, c1, c3, rows013 = call(
        "far", far_body, [shape(256, 384)] * 3 + [shape(8, 768, dtype=F32)],
        (group, g1, g3, far, l0, l1, l3), sc,
    )
    n2, c2, row2, keep_a, send_a, keep_b, send_b, own_pair = call(
        "last", last_body,
        [shape(256, 640), shape(256, 384), shape(8, 256, dtype=F32)]
        + [shape(192, d, dtype=F32), shape(192, d), shape(256, d, dtype=F32), shape(256, d), shape(128, d, dtype=F32)],
        (*groups, near_mine, other, far, c0, c1, c3, part), sc,
    )
    got_a, got_b = swap(send_a), swap(send_b)

    def sent(name, at, near, cf, after):
        return call(
            name, functools.partial(image_body, at), [shape(264, d)],
            (near, cf, far, rows013), (), after,
        )[0]

    p1 = sent("image1", 1, t1, c1, (send_a,))
    p3 = sent("image3", 2, t3, c3, (p1,))
    p2 = call(
        "image2", last_image_body, [shape(264, d)], (n2, c2, near_mine, other, far, row2), (), (p3,)
    )[0]
    z1 = call("step1", step1_body, [shape(192, d)], (keep_a, got_a), (), (p2, got_b))[0]
    w = ring(z1, -2)
    r1, r3, r2 = second(p1, -1), second(p3, -3), second(p2, -2)
    p0 = call(
        "own_image", own_image_body, [shape(256, d, dtype=F32)], (t0, c0, far), (), (z1,)
    )[0]
    two, one = call("step2", step2_body, [shape(128, d)] * 2, (keep_b, got_b, w), (), (p0,))
    v2, v1 = ring(two, -2), ring(one, -1)
    own_img, own_loss, m1, m2, m3 = call(
        "merge_img", merge_img_body,
        [shape(rows, d, dtype=F32), shape(8, 256, dtype=F32)] + [shape(rows + 8, d)] * 3,
        (p0, rows013, r1, r2, r3), (), (one,),
    )
    q1, q3, q2 = first(m1, -1), first(m3, -3), first(m2, -2)
    z3 = call("step3", step3_body, [shape(64, d)], (own_pair, v1, v2), (), (m3,))[0]
    got_c = swap(z3)
    grad_img, grad_txt, loss_out = call(
        "finish", finish_body,
        [shape(rows, d, dtype=F32), shape(rows, d, dtype=F32), shape(1, rows, dtype=F32)],
        (own_img, own_loss, q1, q2, q3, picture, img_inv, own_pair, v1, v2, got_c, caption, txt_inv),
    )
    return grad_img, grad_txt, loss_out.reshape(rows)


def solution(mesh):
    torus = Mesh(mesh.devices.reshape(NX, NC, NZ, NY), AXES)
    return jax.shard_map(
        on_device,
        mesh=torus,
        in_specs=(P(AXES, None), P(AXES, None), P(), P()),
        out_specs=(P(AXES, None), P(AXES, None), P(AXES)),
        check_vma=False,
    )
```
